32 devices in a mesh: segment: 2 (over core), space: 4 (over z), dp: 4 (over y, x).
Axes of the slice: x: 2, y: 2, z: 4, core: 2. Of those that a mesh axis runs over, the one named last changes fastest.
Arguments:
- video_clips: bfloat16 [8, 4, 8, 320, 128], P('dp', None, 'space'), may hold values from -6 to 6
- output_grad: bfloat16 [8, 4, 8, 320, 128], P('dp', None, 'space'), may hold values from -0.3125 to 0.3125
- norm_gain: float32 [2, 320], P('segment'), may hold values from 0.25 to 1.75
- conv_weight: bfloat16 [2, 3, 3, 320, 320], P('segment'), may hold values from -0.109375 to 0.109375
- time_weight: bfloat16 [2, 3, 320, 320], P('segment'), may hold values from -0.1875 to 0.1875
Outputs:
- grad_conv: float32 [2, 3, 3, 320, 320], P('segment')
- grad_time: float32 [2, 3, 320, 320], P('segment')
- grad_gain: float32 [2, 320], P('segment')
The draws below stay inside these ranges and needn't reach their ends.
All inputs are finite; a program needn't handle non-finite values.
Results may differ from the reference program's by a relative error of at most 0.008.
Values may be sent and summed in bfloat16 or wider, within the bound.
A program may use at most 128 MiB of HBM per device.

```python
import jax
import jax.numpy as jnp
from jax import lax

C = 320
F = 4
W = 128
H = 8
CLIPS = 8
SEGMENTS = 2


def level_of(key, dims, pieces, smallest, largest):
    gain, own = 1.0, jax.random.fold_in(key, 6)
    for axis_at, parts in pieces:
        steps = jnp.exp(jax.random.uniform(jax.random.fold_in(own, axis_at), (parts,), jnp.float32, smallest / len(pieces), largest / len(pieces)))
        gain = gain * jnp.repeat(steps, dims[axis_at] // parts).reshape([-1 if axis == axis_at else 1 for axis in range(len(dims))])
    return gain


def centred(stream_key, extent, deviation, limit, shards=(), dtype=jnp.bfloat16):
    factor_of = level_of(stream_key, extent, shards, -0.22, 0.18) if shards else 1.0
    result = jax.random.normal(stream_key, extent, jnp.float32) * deviation * factor_of
    return jnp.minimum(jnp.maximum(result, -limit), limit).astype(dtype)


def setup_inputs(seed: int = 0) -> dict:
    streams_of = jax.random.split(jax.random.key(seed), 6)
    return {
        "video_clips": centred(streams_of[0], (CLIPS, F, H, C, W), 1.0, 6.0, ((0, 4), (2, 4))),
        "output_grad": centred(streams_of[1], (CLIPS, F, H, C, W), (4.0 / (CLIPS * F * H * W) ** 0.5), 0.3125, ((0, 4), (2, 4))),
        "norm_gain": jnp.clip(1.0 + 0.15 * jax.random.normal(streams_of[2], (SEGMENTS, C), jnp.float32), 0.25, 1.75),
        "conv_weight": centred(streams_of[3], (SEGMENTS, 3, 3, C, C), (9 * C) ** -0.5, 0.109375, ((0, 2),)),
        "time_weight": centred(streams_of[4], (SEGMENTS, 3, C, C), (3 * C) ** -0.5, 0.1875, ((0, 2),)),
    }


EPS = 1e-06

def shift_cols(values, offset):
    if offset == 0:
        return values
    zero_col = jnp.zeros_like(values[..., :1])
    if offset > 0:
        return jnp.concatenate([values[..., 1:], zero_col], axis=-1)
    return jnp.concatenate([zero_col, values[..., :-1]], axis=-1)

def shift_frames(values, offset):
    if offset == 0:
        return values
    zero_frame = jnp.zeros_like(values[:1])
    if offset > 0:
        return jnp.concatenate([values[1:], zero_frame], axis=0)
    return jnp.concatenate([zero_frame, values[:-1]], axis=0)

def pad_rows(values):
    return jnp.pad(values, ((0, 0), (1, 1), (0, 0), (0, 0)))

def norm_terms(merged, gain_row):
    widened = merged.astype(jnp.float32)
    scale = lax.rsqrt(lax.optimization_barrier(jnp.mean(widened * widened, axis=2, keepdims=True)) + EPS)
    return (widened, scale, widened * scale * gain_row[None, None, :, None])

def silu_slope(values):
    sigma = jax.nn.sigmoid(values)
    return sigma * (1.0 + values * (1.0 - sigma))

def spatial_conv(padded, kernel):
    height = padded.shape[1] - 2
    widened = padded.astype(jnp.float32)
    terms = []
    for row_tap in range(3):
        band = widened[:, row_tap:row_tap + height]
        for col_tap in range(3):
            terms.append(jnp.einsum('fhcw,co->fhow', shift_cols(band, col_tap - 1), kernel[row_tap, col_tap].astype(jnp.float32)))
    return sum(terms)

def temporal_conv(act_two, tkernel):
    widened = act_two.astype(jnp.float32)
    terms = [jnp.einsum('fhcw,co->fhow', shift_frames(widened, frame_tap - 1), tkernel[frame_tap].astype(jnp.float32)) for frame_tap in range(3)]
    return sum(terms)

def section_forward(merged, gain_row, kernel, tkernel):
    widened, scale, pre = norm_terms(merged, gain_row)
    act_one = jax.nn.silu(pre).astype(jnp.bfloat16)
    padded = pad_rows(act_one)
    hidden = spatial_conv(padded, kernel).astype(jnp.bfloat16)
    act_two = jax.nn.silu(hidden.astype(jnp.float32)).astype(jnp.bfloat16)
    output = (widened + temporal_conv(act_two, tkernel)).astype(jnp.bfloat16)
    return (output, hidden, padded)

def section_backward(merged, padded, hidden, grad_out, grad_skip, gain_row, kernel, tkernel):
    height = hidden.shape[1]
    hidden_wide = hidden.astype(jnp.float32)
    act_two = jax.nn.silu(hidden_wide).astype(jnp.bfloat16).astype(jnp.float32)
    grad_wide = grad_out.astype(jnp.float32)
    grad_time = jnp.stack([jnp.einsum('fhcw,fhow->co', shift_frames(act_two, frame_tap - 1), grad_wide) for frame_tap in range(3)])
    grad_act_two = sum([jnp.einsum('fhow,co->fhcw', shift_frames(grad_wide, 1 - frame_tap), tkernel[frame_tap].astype(jnp.float32)) for frame_tap in range(3)])
    grad_hidden = (grad_act_two * silu_slope(hidden_wide) + grad_skip.astype(jnp.float32)).astype(jnp.bfloat16)
    grad_pad = pad_rows(grad_hidden).astype(jnp.float32)
    grad_hidden_wide = grad_hidden.astype(jnp.float32)
    padded_wide = padded.astype(jnp.float32)
    conv_rows = []
    grad_terms = []
    for row_tap in range(3):
        band = padded_wide[:, row_tap:row_tap + height]
        back_band = grad_pad[:, 2 - row_tap:2 - row_tap + height]
        conv_cols = []
        for col_tap in range(3):
            conv_cols.append(jnp.einsum('fhcw,fhow->co', shift_cols(band, col_tap - 1), grad_hidden_wide))
            grad_terms.append(jnp.einsum('fhow,co->fhcw', shift_cols(back_band, 1 - col_tap), kernel[row_tap, col_tap].astype(jnp.float32)))
        conv_rows.append(jnp.stack(conv_cols))
    grad_conv = jnp.stack(conv_rows)
    widened, scale, pre = norm_terms(merged, gain_row)
    grad_pre = sum(grad_terms) * silu_slope(pre)
    grad_gain = lax.optimization_barrier(jnp.sum(grad_pre * widened * scale, axis=(0, 1, 3)))
    weighted = grad_pre * gain_row[None, None, :, None]
    grad_merged = weighted * scale - widened * scale * scale * scale * lax.optimization_barrier(jnp.mean(weighted * widened, axis=2, keepdims=True))
    grad_in = (grad_wide + grad_merged).astype(jnp.bfloat16)
    return (grad_in, grad_conv, grad_time, grad_gain)

def reference(video_clips, output_grad, norm_gain, conv_weight, time_weight):
    sections = conv_weight.shape[0]
    half_point = sections // 2

    def one_clip(totals, inputs):
        clip_in, clip_grad = inputs
        current = clip_in
        saved = []
        skips = []
        for section in range(sections):
            if section >= half_point:
                merged = (current.astype(jnp.float32) + skips[sections - 1 - section].astype(jnp.float32)).astype(jnp.bfloat16)
            else:
                merged = current
            output, hidden, padded = section_forward(merged, norm_gain[section], conv_weight[section], time_weight[section])
            if section < half_point:
                skips.append(hidden)
            saved.append((merged, padded, hidden))
            current = output
        grad_now = clip_grad
        skip_grads = [None] * sections
        conv_parts = [None] * sections
        time_parts = [None] * sections
        gain_parts = [None] * sections
        for section in reversed(range(sections)):
            merged, padded, hidden = saved[section]
            if section < half_point:
                grad_skip = skip_grads[section]
            else:
                grad_skip = jnp.zeros_like(hidden)
            grad_in, grad_conv, grad_time, grad_gain = section_backward(merged, padded, hidden, grad_now, grad_skip, norm_gain[section], conv_weight[section], time_weight[section])
            if section >= half_point:
                skip_grads[sections - 1 - section] = grad_in
            conv_parts[section] = grad_conv
            time_parts[section] = grad_time
            gain_parts[section] = grad_gain
            grad_now = grad_in
        return ((totals[0] + jnp.stack(conv_parts), totals[1] + jnp.stack(time_parts), totals[2] + jnp.stack(gain_parts)), None)
    initial = (jnp.zeros(conv_weight.shape, jnp.float32), jnp.zeros(time_weight.shape, jnp.float32), jnp.zeros(norm_gain.shape, jnp.float32))
    totals, _ = lax.scan(one_clip, initial, (video_clips, output_grad))
    return (totals[0], totals[1], totals[2])
```

```python
import functools
import types

import jax
import jax.numpy as jnp
from jax import lax
from jax.experimental import pallas as pl
from jax.experimental.pallas import tpu as pltpu
from jax.sharding import PartitionSpec as P

EPS = 1e-06
MESH = pl.DeviceIdType.MESH
VMEM = pl.BlockSpec(memory_space=pltpu.VMEM)
ANY = pl.BlockSpec(memory_space=pl.ANY)
BF16 = jnp.bfloat16
F32 = jnp.float32
LIMIT = 65000 * 1024
NT = (((1,), (1,)), ((), ()))
LANES = 128
BANDS = 4


def sigmoid(values):
    return 0.5 + 0.5 * jnp.tanh(0.5 * values)


def slope(values):
    sig = sigmoid(values)
    return sig * (1.0 + values * (1.0 - sig))


def shifted(values, offset):
    column = lax.broadcasted_iota(jnp.int32, values.shape, 1)
    if offset > 0:
        return jnp.where(column < LANES - 1, pltpu.roll(values, LANES - 1, 1), 0.0)
    return jnp.where(column > 0, pltpu.roll(values, 1, 1), 0.0)


def lanes_at(start, size):
    return pl.ds(pl.multiple_of(start, LANES), size)


def rows_at(start, size):
    return pl.ds(pl.multiple_of(start, 16), size)


def unit_rows(channels, groups, places):
    total = 3 * channels * channels // LANES
    return -(-total // (2 * groups * places * 16)) * 16


def scratch_of(frames, height, channels, groups, places):
    fw = frames * LANES
    cols = height * fw
    taps = 3 * channels
    unit = unit_rows(channels, groups, places)
    piece = places * unit
    half = groups * piece
    dma = pltpu.SemaphoreType.DMA
    return {
        "u": pltpu.VMEM((frames, height, channels, LANES), BF16),
        "m1": pltpu.VMEM((channels, cols), BF16),
        "hid": pltpu.VMEM((2, channels, cols), BF16),
        "xs": pltpu.VMEM((2, taps, cols + 2 * fw), BF16),
        "ghs": pltpu.VMEM((2, taps, cols + 2 * fw), BF16),
        "act2": pltpu.VMEM((2, taps, cols), BF16),
        "gs": pltpu.VMEM((2, taps, cols), BF16),
        "conv": pltpu.VMEM((channels, cols), F32),
        "ga": pltpu.VMEM((channels, cols), F32),
        "wr": pltpu.VMEM((2, 3, taps, channels), BF16),
        "tr": pltpu.VMEM((2, taps, channels), BF16),
        "ws": pltpu.VMEM((2, 3, channels, taps), BF16),
        "ts": pltpu.VMEM((2, channels, taps), BF16),
        "grow": pltpu.VMEM((2, 1, channels), F32),
        "gcol": pltpu.VMEM((2, channels, LANES), F32),
        "ggain": pltpu.VMEM((2, channels, LANES), F32),
        "g": pltpu.VMEM((2, BANDS, 2 * half, LANES), BF16),
        "pair": pltpu.VMEM((2, BANDS, half, LANES), BF16),
        "got_dp": pltpu.VMEM((2, BANDS, groups - 1, piece, LANES), BF16),
        "part": pltpu.VMEM((2, BANDS, piece, LANES), BF16),
        "got_sp": pltpu.VMEM((2, BANDS, places - 1, unit, LANES), BF16),
        "done": pltpu.VMEM((2, BANDS, piece, LANES), BF16),
        "gain_now": pltpu.VMEM((3, 8, channels), F32),
        "gain_pair": pltpu.VMEM((8, channels), F32),
        "gain_dp": pltpu.VMEM((groups - 1, 8, channels), F32),
        "gain_sp": pltpu.VMEM((places - 1, 8, channels), F32),
        "in_sem": dma((frames,)),
        "own_sem": dma((3,)),
        "out_sem": dma((3,)),
        "there_sem": dma((3,)),
        "gout_sem": dma((3,)),
        "halo_send": dma((2, 2, 2, frames)),
        "halo_recv": dma((2, 2, 2, frames)),
        "send": dma((5, 2, BANDS)),
        "recv": dma((5, 2, BANDS)),
        "keep": dma((2, BANDS)),
        "gain_send": dma((3,)),
        "gain_recv": dma((3,)),
    }


def step_kernel(names, clips, outgrad, gain, w, t, whole, gain_out, *refs):
    v = types.SimpleNamespace(**dict(zip(names, refs)))
    _, frames, height, channels, _ = clips.shape
    fw = frames * LANES
    cols = height * fw
    pairs = frames // 2
    me = lax.axis_index("segment")
    group, groups = lax.axis_index("dp"), lax.axis_size("dp")
    place, places = lax.axis_index("space"), lax.axis_size("space")
    has_up, has_down = place > 0, place < places - 1
    other = {"segment": 1 - me}
    dp_peers = [{"dp": (group + k) % groups} for k in range(1, groups)]
    cross_peers = [
        {"dp": (group + k) % groups, "segment": 1 - me} for k in range(1, groups)
    ]
    sp_peers = [{"space": (place + k) % places} for k in range(1, places)]
    center = slice(channels, 2 * channels)

    def remote(src, dst, send, recv, target):
        return pltpu.make_async_remote_copy(
            src_ref=src, dst_ref=dst, send_sem=send, recv_sem=recv,
            device_id=target, device_id_type=MESH,
        )

    barrier = pltpu.get_barrier_semaphore()
    partners = [other] + dp_peers + cross_peers + sp_peers
    for target in partners:
        pl.semaphore_signal(barrier, inc=1, device_id=target, device_id_type=MESH)

    def clip_copy(f):
        return pltpu.make_async_copy(clips.at[me, f], v.u.at[f], v.in_sem.at[f])

    for f in range(frames):
        clip_copy(f).start()
    own_copies = [
        pltpu.make_async_copy(w, v.wr.at[me], v.own_sem.at[0]),
        pltpu.make_async_copy(t, v.tr.at[me], v.own_sem.at[1]),
        pltpu.make_async_copy(gain, v.grow.at[me], v.own_sem.at[2]),
    ]
    for copy in own_copies[::-1]:
        copy.start()

    for row in range(height):
        first, last = row * fw, row * fw + fw - LANES
        for s in range(2):
            v.act2[s, 0:channels, first : first + LANES] = jnp.zeros((channels, LANES), BF16)
            v.act2[s, 2 * channels :, last : last + LANES] = jnp.zeros((channels, LANES), BF16)
            v.gs[s, 0:channels, last : last + LANES] = jnp.zeros((channels, LANES), BF16)
            v.gs[s, 2 * channels :, first : first + LANES] = jnp.zeros((channels, LANES), BF16)

    @pl.when(jnp.logical_not(has_up))
    def _():
        for s in range(2):
            v.xs[s, center, 0:fw] = jnp.zeros((channels, fw), BF16)
            v.ghs[s, center, 0:fw] = jnp.zeros((channels, fw), BF16)

    @pl.when(jnp.logical_not(has_down))
    def _():
        for s in range(2):
            v.xs[s, center, cols + fw :] = jnp.zeros((channels, fw), BF16)
            v.ghs[s, center, cols + fw :] = jnp.zeros((channels, fw), BF16)

    used = 3 * channels * channels // LANES
    if used < v.g.shape[2]:
        for s in range(2):
            for band in range(BANDS):
                v.g[s, band, used:] = jnp.zeros((v.g.shape[2] - used, LANES), BF16)
    v.ggain[...] = jnp.zeros(v.ggain.shape, F32)

    pl.semaphore_wait(barrier, len(partners))
    there = [
        remote(gain, v.grow.at[me], v.out_sem.at[2], v.there_sem.at[2], other),
        remote(w, v.wr.at[me], v.out_sem.at[0], v.there_sem.at[0], other),
        remote(t, v.tr.at[me], v.out_sem.at[1], v.there_sem.at[1], other),
    ]
    for copy in there:
        copy.start()
    for k in range(3):
        for f in range(frames):
            at = f + k - 1
            if 0 <= at < frames:
                for row in range(height):
                    lane = row * fw + at * LANES
                    pltpu.make_async_copy(
                        outgrad.at[me, f, row],
                        v.gs.at[1, k * channels : (k + 1) * channels, lane : lane + LANES],
                        v.gout_sem.at[k],
                    ).start()

    def wait_outgrad():
        for k in range(3):
            size = height * (frames - (k != 1)) * LANES
            ref = v.gs.at[1, k * channels : (k + 1) * channels, 0:size]
            pltpu.make_async_copy(ref, ref, v.gout_sem.at[k]).wait()

    def put_row(store, s, row, f, values, reverse, own):
        lane = lanes_at(row * fw + f * LANES, LANES)
        for tap in range(3):
            offset = 1 - tap if reverse else tap - 1
            rows = slice(tap * channels, (tap + 1) * channels)
            if offset:
                store[s, rows, lane] = shifted(values, offset).astype(BF16)
            elif own:
                store[s, rows, lane] = values.astype(BF16)

    def put_frames(store, s, row, f, tile, sign):
        for k in (1, 0, 2):
            at = f + sign * (k - 1)

            def put(k=k, at=at):
                lane = lanes_at(row * fw + at * LANES, LANES)
                store[s, k * channels : (k + 1) * channels, lane] = tile

            if k == 1:
                put()
            else:
                pl.when((at >= 0) & (at < frames))(put)

    def halo_copy(store, kind, s, f, down):
        from_row, into_row = (height, 0) if down else (1, height + 1)
        return remote(
            store.at[s, center, lanes_at(from_row * fw + f * LANES, LANES)],
            store.at[s, center, lanes_at(into_row * fw + f * LANES, LANES)],
            v.halo_send.at[kind, s, down, f],
            v.halo_recv.at[kind, s, down, f],
            {"space": place + 1} if down else {"space": place - 1},
        )

    def halo_start(store, kind, s, f):
        pl.when(has_up)(lambda: halo_copy(store, kind, s, f, 0).start())
        pl.when(has_down)(lambda: halo_copy(store, kind, s, f, 1).start())

    def halo_take(store, kind, s, f, reverse):
        pl.when(has_up)(lambda: halo_copy(store, kind, s, f, 1).wait_recv())
        pl.when(has_down)(lambda: halo_copy(store, kind, s, f, 0).wait_recv())
        for row in (0, height + 1):
            lane = lanes_at(row * fw + f * LANES, LANES)
            values = store[s, center, lane].astype(F32)
            put_row(store, s, row, f, values, reverse, False)

    def halo_sent(store, kind, s):
        def body(f, _):
            pl.when(has_up)(lambda: halo_copy(store, kind, s, f, 0).wait_send())
            pl.when(has_down)(lambda: halo_copy(store, kind, s, f, 1).wait_send())
            return 0

        lax.fori_loop(0, frames, body, 0)

    def conv_own(store, s, reverse):
        above, below = (2, 0) if reverse else (0, 2)
        slot = 1 - s if reverse else s
        v.conv[...] = jnp.dot(
            v.ws[slot, 1], store[s, :, fw : fw + cols], preferred_element_type=F32
        )
        if height > 1:
            v.conv[:, fw:] += jnp.dot(
                v.ws[slot, above], store[s, :, fw:cols], preferred_element_type=F32
            )
            v.conv[:, : cols - fw] += jnp.dot(
                v.ws[slot, below], store[s, :, 2 * fw : cols + fw], preferred_element_type=F32
            )

    def conv_rest(store, s, row, p, reverse):
        above, below = (2, 0) if reverse else (0, 2)
        slot = 1 - s if reverse else s
        wide = 2 * LANES
        total = v.conv[:, lanes_at(row * fw + p * wide, wide)]
        if row == 0:
            total += jnp.dot(
                v.ws[slot, above], store[s, :, lanes_at(p * wide, wide)],
                preferred_element_type=F32,
            )
        if row == height - 1:
            total += jnp.dot(
                v.ws[slot, below], store[s, :, lanes_at(cols + fw + p * wide, wide)],
                preferred_element_type=F32,
            )
        return total

    def norm(s, merged):
        scale = lax.rsqrt(jnp.mean(merged * merged, axis=0, keepdims=True) + EPS)
        return scale, merged * scale * v.gcol[s]

    def activate(s, row, f, merged):
        _, pre = norm(s, merged)
        put_row(v.xs, s, row + 1, f, pre * sigmoid(pre), False, True)

    def hidden_of(s):
        def body(p, _):
            for q in range(2):
                halo_take(v.xs, 0, s, 2 * p + q, False)
            for row in range(height):
                hidden = conv_rest(v.xs, s, row, p, False).astype(BF16)
                v.hid[s, :, lanes_at(row * fw + p * 2 * LANES, 2 * LANES)] = hidden
                wide = hidden.astype(F32)
                act = (wide * sigmoid(wide)).astype(BF16)
                for q in range(2):
                    tile = act[:, q * LANES : (q + 1) * LANES]
                    put_frames(v.act2, s, row, 2 * p + q, tile, -1)
            return 0

        lax.fori_loop(0, pairs, body, 0)

    def transpose_weights(s):
        def body(tap, _):
            v.ws[s, tap] = v.wr[s, tap].T
            return 0

        lax.fori_loop(0, 3, body, 0)
        if s == 0:
            v.ts[0] = v.tr[0].T

    def join_weights(s):
        def body(tap, _):
            for j in range(3):
                own = slice(j * channels, (j + 1) * channels)
                v.ws[1 - s, tap, :, own] = v.wr[s, tap, own]
            return 0

        lax.fori_loop(0, 3, body, 0)
        for j in range(3):
            own = slice(j * channels, (j + 1) * channels)
            v.ts[1 - s, :, own] = v.tr[s, own]

    unit = unit_rows(channels, groups, places)
    piece = places * unit
    half = groups * piece
    PAIR, DP, SP, BACK_SP, BACK_DP = range(5)

    def sems(stage, s, band):
        return v.send.at[stage, s, band], v.recv.at[stage, s, band]

    def pair_copy(s, band):
        return remote(
            v.g.at[s, band, rows_at((1 - me) * half, half)], v.pair.at[s, band],
            *sems(PAIR, s, band), other,
        )

    def piece_rows(d):
        return rows_at((me * groups + d) * piece, piece)

    def step_pair(s, band):
        pair_copy(s, band).wait_recv()
        own = rows_at(me * half, half)
        v.g[s, band, own] = (
            v.g[s, band, own].astype(F32) + v.pair[s, band].astype(F32)
        ).astype(BF16)
        for k in range(1, groups):
            remote(
                v.g.at[s, band, piece_rows((group + k) % groups)],
                v.got_dp.at[s, band, k - 1], *sems(DP, s, band), dp_peers[k - 1],
            ).start()

    def all_dp(s, band):
        return remote(
            v.got_dp.at[s, band], v.got_dp.at[s, band], *sems(DP, s, band), dp_peers[0]
        )

    def step_dp(s, band):
        all_dp(s, band).wait_recv()
        total = v.g[s, band, piece_rows(group)].astype(F32)
        for k in range(groups - 1):
            total += v.got_dp[s, band, k].astype(F32)
        v.part[s, band] = total.astype(BF16)
        for k in range(1, places):
            remote(
                v.part.at[s, band, rows_at(((place + k) % places) * unit, unit)],
                v.got_sp.at[s, band, k - 1], *sems(SP, s, band), sp_peers[k - 1],
            ).start()

    def all_sp(stage, s, band):
        return remote(
            v.got_sp.at[s, band], v.got_sp.at[s, band], *sems(stage, s, band), sp_peers[0]
        )

    def step_sp(s, band):
        all_sp(SP, s, band).wait_recv()
        own = rows_at(place * unit, unit)
        total = v.part[s, band, own].astype(F32)
        for k in range(places - 1):
            total += v.got_sp[s, band, k].astype(F32)
        v.done[s, band, own] = total.astype(BF16)
        for k in range(1, places):
            remote(
                v.done.at[s, band, own], v.done.at[s, band, own],
                *sems(BACK_SP, s, band), sp_peers[k - 1],
            ).start()

    def home_copy(s, band, target):
        return remote(
            v.done.at[s, band], whole.at[band, piece_rows(group)],
            *sems(BACK_DP, s, band), target,
        )

    def keep_copy(s, band):
        return pltpu.make_async_copy(
            v.done.at[s, band], whole.at[band, piece_rows(group)], v.keep.at[s, band]
        )

    def step_back(s, band):
        all_sp(BACK_SP, s, band).wait_recv()

        @pl.when(me == s)
        def _():
            for target in dp_peers:
                home_copy(s, band, target).start()
            keep_copy(s, band).start()

        @pl.when(me != s)
        def _():
            for target in cross_peers + [other]:
                home_copy(s, band, target).start()

    def step_home(s, band):
        @pl.when(me == s)
        def _():
            keep_copy(s, band).wait()
            count = (2 * groups - 1) * piece
            ref = whole.at[band, 0:count]
            remote(ref, ref, *sems(BACK_DP, s, band), other).wait_recv()

    def wait_sends(s):
        def body(band, _):
            pair_copy(s, band).wait_send()
            all_dp(s, band).wait_send()
            all_sp(SP, s, band).wait_send()
            all_sp(BACK_SP, s, band).wait_send()
            @pl.when(me == s)
            def _():
                ref = whole.at[band, 0 : (groups - 1) * piece]
                remote(ref, ref, *sems(BACK_DP, s, band), other).wait_send()

            @pl.when(me != s)
            def _():
                ref = whole.at[band, 0 : groups * piece]
                remote(ref, ref, *sems(BACK_DP, s, band), other).wait_send()

            return 0

        lax.fori_loop(0, BANDS, body, 0)

    def store_band(s, band, j, values):
        tiles, cut = channels // LANES, channels // 2
        base = j * (channels * channels // LANES)
        for n in range(tiles):
            v.g[s, band, base + n * channels : base + (n + 1) * channels] = values[
                :, n * LANES : (n + 1) * LANES
            ].astype(BF16)
        last = values[:, tiles * LANES :]
        v.g[s, band, base + tiles * channels : base + tiles * channels + cut] = jnp.concatenate(
            [last[:cut], last[cut:]], axis=1
        ).astype(BF16)

    def grads_of(s):
        for j in range(3):
            own = slice(j * channels, (j + 1) * channels)
            store_band(
                s, 0, j,
                lax.dot_general(v.act2[s, own], v.gs[s, center], NT, preferred_element_type=F32),
            )
        pair_copy(s, 0).start()

        def body(i, _):
            for j in range(3):
                own = slice(j * channels, (j + 1) * channels)
                store_band(
                    s, 1 + i, j,
                    lax.dot_general(
                        v.xs[s, own, lanes_at(i * fw, cols)],
                        v.ghs[s, center, fw : fw + cols], NT, preferred_element_type=F32,
                    ),
                )
            pair_copy(s, 1 + i).start()
            step_pair(s, i)
            return 0

        lax.fori_loop(0, 3, body, 0)

    def through_time(s):
        v.ga[...] = jnp.dot(v.ts[1 - s], v.gs[s], preferred_element_type=F32)

    def ghidden_of(s):
        def body(f, _):
            for row in range(height):
                lane = lanes_at(row * fw + f * LANES, LANES)
                gh = v.ga[:, lane] * slope(v.hid[s, :, lane].astype(F32))
                if s == 0:
                    gh = gh + v.gs[s, center, lane].astype(F32)
                put_row(v.ghs, s, row + 1, f, gh, True, True)
            halo_start(v.ghs, 1, s, f)
            return 0

        lax.fori_loop(0, frames, body, 0)

    def input_grads(s, p):
        for q in range(2):
            halo_take(v.ghs, 1, s, 2 * p + q, True)
        for row in range(height):
            total = conv_rest(v.ghs, s, row, p, True)
            for q in range(2):
                f = 2 * p + q
                lane = lanes_at(row * fw + f * LANES, LANES)
                merged = (v.m1[:, lane] if s else v.u[f, row]).astype(F32)
                scale, pre = norm(s, merged)
                gpre = total[:, q * LANES : (q + 1) * LANES] * slope(pre)
                v.ggain[s] += gpre * merged * scale
                if s:
                    weighted = gpre * v.gcol[s]
                    gm = weighted * scale - merged * (scale * scale * scale) * jnp.mean(
                        weighted * merged, axis=0, keepdims=True
                    )
                    gin = (v.gs[s, center, lane].astype(F32) + gm).astype(BF16)
                    put_frames(v.gs, 0, row, f, gin, 1)

    own_copies[2].wait()
    there[0].wait_recv()
    for s in range(2):
        v.gcol[s] = jnp.broadcast_to(v.grow[s], (LANES, channels)).T

    def enter(f, _):
        clip_copy(f).wait()
        for row in range(height):
            activate(0, row, f, v.u[f, row].astype(F32))
        halo_start(v.xs, 0, 0, f)
        return 0

    lax.fori_loop(0, frames, enter, 0)
    for copy in own_copies[:2]:
        copy.wait()
    for copy in there[1:]:
        copy.wait_recv()
    transpose_weights(0)
    conv_own(v.xs, 0, False)
    transpose_weights(1)
    hidden_of(0)

    def pass_on(p, _):
        for row in range(height):
            at = row * fw + p * 2 * LANES
            mixed = jnp.dot(
                v.ts[0], v.act2[0, :, lanes_at(at, 2 * LANES)], preferred_element_type=F32
            )
            for q in range(2):
                f = 2 * p + q
                lane = lanes_at(at + q * LANES, LANES)
                out = v.u[f, row].astype(F32) + mixed[:, q * LANES : (q + 1) * LANES]
                out = out.astype(BF16).astype(F32)
                merged = (out + v.hid[0, :, lane].astype(F32)).astype(BF16)
                v.m1[:, lane] = merged
                activate(1, row, f, merged.astype(F32))
        for q in range(2):
            halo_start(v.xs, 0, 1, 2 * p + q)
        return 0

    lax.fori_loop(0, pairs, pass_on, 0)
    conv_own(v.xs, 1, False)
    join_weights(1)
    wait_outgrad()
    through_time(1)
    hidden_of(1)

    ghidden_of(1)
    grads_of(1)
    join_weights(0)
    conv_own(v.ghs, 1, True)
    step_pair(1, 3)
    step_dp(1, 0)
    step_dp(1, 1)

    def back_up(p, _):
        input_grads(1, p)
        step_dp(1, 2 + p)
        step_sp(1, p)
        return 0

    lax.fori_loop(0, 2, back_up, 0)

    through_time(0)
    step_sp(1, 2)
    step_sp(1, 3)
    ghidden_of(0)
    step_back(1, 0)
    step_back(1, 1)
    grads_of(0)
    step_pair(0, 3)
    step_back(1, 2)
    step_back(1, 3)
    step_dp(0, 0)
    conv_own(v.ghs, 0, True)
    step_dp(0, 1)
    step_dp(0, 2)
    step_dp(0, 3)

    def back_down(p, _):
        input_grads(0, p)
        step_sp(0, 2 * p)
        step_sp(0, 2 * p + 1)
        return 0

    lax.fori_loop(0, 2, back_down, 0)

    ones = jnp.ones((8, LANES), F32)
    sums = [
        lax.dot_general(
            ones, v.ggain[s], NT, precision=lax.Precision.HIGHEST, preferred_element_type=F32
        )
        for s in range(2)
    ]
    line = lax.broadcasted_iota(jnp.int32, sums[0].shape, 0)
    v.gain_now[0] = jnp.where(line == 0, sums[0], sums[1])
    gain_pair = remote(
        v.gain_now.at[0], v.gain_pair, v.gain_send.at[0], v.gain_recv.at[0], other
    )
    gain_pair.start()
    step_back(0, 0)
    step_back(0, 1)
    gain_pair.wait_recv()
    v.gain_now[1] = v.gain_now[0] + v.gain_pair[...]
    for k in range(groups - 1):
        remote(
            v.gain_now.at[1], v.gain_dp.at[k], v.gain_send.at[1], v.gain_recv.at[1], dp_peers[k]
        ).start()
    step_back(0, 2)
    step_back(0, 3)
    gain_dp = remote(
        v.gain_dp, v.gain_dp, v.gain_send.at[1], v.gain_recv.at[1], dp_peers[0]
    )
    gain_dp.wait_recv()
    total = v.gain_now[1]
    for k in range(groups - 1):
        total += v.gain_dp[k]
    v.gain_now[2] = total
    for k in range(places - 1):
        remote(
            v.gain_now.at[2], v.gain_sp.at[k], v.gain_send.at[2], v.gain_recv.at[2], sp_peers[k]
        ).start()
    gain_sp = remote(
        v.gain_sp, v.gain_sp, v.gain_send.at[2], v.gain_recv.at[2], sp_peers[0]
    )
    for copy in there:
        copy.wait_send()
    for s in range(2):
        halo_sent(v.xs, 0, s)
        halo_sent(v.ghs, 1, s)
        wait_sends(s)
    gain_pair.wait_send()
    gain_dp.wait_send()
    gain_sp.wait()
    for k in range(places - 1):
        total += v.gain_sp[k]
    gain_out[...] = total
    for s in range(2):
        for band in range(BANDS):
            step_home(s, band)


def unpack_kernel(packed, gains, conv, time, gain):
    band = pl.program_id(0)
    channels = conv.shape[1]
    tiles, cut = channels // LANES, channels // 2

    def unpack(into):
        for j in range(3):
            base = j * (channels * channels // LANES)
            rows = slice(j * channels, (j + 1) * channels)
            for n in range(tiles):
                into[rows, n * LANES : (n + 1) * LANES] = packed[
                    0, base + n * channels : base + (n + 1) * channels
                ].astype(F32)
            last = packed[0, base + tiles * channels : base + tiles * channels + cut].astype(F32)
            into[j * channels : j * channels + cut, tiles * LANES :] = last[:, :64]
            into[j * channels + cut : (j + 1) * channels, tiles * LANES :] = last[:, 64:]

    @pl.when(band == 0)
    def _():
        unpack(time)
        me = lax.axis_index("segment")
        gain[...] = jnp.where(me == 0, gains[0:1], gains[1:2])

    @pl.when(band > 0)
    def _():
        unpack(conv)


def body(video_clips, output_grad, norm_gain, conv_weight, time_weight):
    channels = conv_weight.shape[3]
    clips, frames, height, _, width = video_clips.shape
    assert clips == 2 and width == LANES and channels % LANES == 64 and frames == 4
    groups, places = lax.axis_size("dp"), lax.axis_size("space")
    taps = 3 * channels
    scratch = scratch_of(frames, height, channels, groups, places)
    rows = 2 * groups * places * unit_rows(channels, groups, places)
    packed, gains = pl.pallas_call(
        functools.partial(step_kernel, tuple(scratch)),
        out_shape=[
            jax.ShapeDtypeStruct((BANDS, rows, LANES), BF16),
            jax.ShapeDtypeStruct((8, channels), F32),
        ],
        in_specs=[ANY, ANY, VMEM, ANY, ANY],
        out_specs=[VMEM, VMEM],
        scratch_shapes=list(scratch.values()),
        compiler_params=pltpu.CompilerParams(
            collective_id=0, has_side_effects=True, vmem_limit_bytes=LIMIT
        ),
        name="step",
    )(
        video_clips, output_grad, norm_gain,
        conv_weight.reshape(3, taps, channels), time_weight.reshape(taps, channels),
    )
    conv, time, row = pl.pallas_call(
        unpack_kernel,
        grid=(BANDS,),
        out_shape=[
            jax.ShapeDtypeStruct((3 * taps, channels), F32),
            jax.ShapeDtypeStruct((taps, channels), F32),
            jax.ShapeDtypeStruct((1, channels), F32),
        ],
        in_specs=[
            pl.BlockSpec((1, rows, LANES), lambda b: (b, 0, 0)),
            pl.BlockSpec((8, channels), lambda b: (0, 0)),
        ],
        out_specs=[
            pl.BlockSpec((taps, channels), lambda b: (jnp.maximum(b - 1, 0), 0)),
            pl.BlockSpec((taps, channels), lambda b: (0, 0)),
            pl.BlockSpec((1, channels), lambda b: (0, 0)),
        ],
        compiler_params=pltpu.CompilerParams(vmem_limit_bytes=32000 * 1024),
        name="unpack",
    )(packed, gains)
    return (
        conv.reshape(conv_weight.shape),
        time.reshape(time_weight.shape),
        row,
    )


def solution(mesh):
    placed = (
        P("dp", None, "space", None, None),
        P("dp", None, "space", None, None),
        P("segment", None),
        P("segment", None, None, None, None),
        P("segment", None, None, None),
    )
    return jax.shard_map(
        body,
        mesh=mesh,
        in_specs=placed,
        out_specs=(
            P("segment", None, None, None, None),
            P("segment", None, None, None),
            P("segment", None),
        ),
        check_vma=False,
    )
```

```python
import functools
import types

import jax
import jax.numpy as jnp
from jax import lax
from jax.experimental import pallas as pl
from jax.experimental.pallas import tpu as pltpu
from jax.sharding import PartitionSpec as P

EPS = 1e-06
MESH = pl.DeviceIdType.MESH
VMEM = pl.BlockSpec(memory_space=pltpu.VMEM)
ANY = pl.BlockSpec(memory_space=pl.ANY)
BF16 = jnp.bfloat16
F32 = jnp.float32
LIMIT = 65000 * 1024
NT = (((1,), (1,)), ((), ()))
LANES = 128
BANDS = 4


ROUTES = (("direct",) * 4, ("direct",) * 4)
DURING = {
    "grads1": [[(0, 1, 0)], [(0, 1, 1)], [(0, 1, 2)]],
    "joined": [],
    "conv1": [(0, 1, 3)],
    "up": [[(1, 1, 0), (1, 1, 1)], [(1, 1, 2)]],
    "time0": [(1, 1, 3)],
    "ghidden0": [(2, 1, 0)],
    "grads0": [[(2, 1, 1), (2, 1, 2)], [(0, 0, 0), (2, 1, 3)], [(0, 0, 1), (3, 1, 0)]],
}
LAST = [
    "conv", (0, 0, 2), (3, 1, 1), (0, 0, 3), (1, 0, 0), (3, 1, 2), "rest0", (1, 0, 1), "rest1",
    (3, 1, 3), (1, 0, 2), (4, 1, 0), "gain0", (1, 0, 3), (4, 1, 1), (2, 0, 0), (4, 1, 2), (2, 0,
    1), "gain1", (2, 0, 2), (4, 1, 3), (5, 1, 0), (2, 0, 3), (3, 0, 0), (5, 1, 1), "gain2", (3,
    0, 1), (5, 1, 2), (3, 0, 2), (5, 1, 3), (3, 0, 3), (4, 0, 0), "gain3", (4, 0, 1), (4, 0, 2),
    (4, 0, 3), (5, 0, 0), (5, 0, 1), (5, 0, 2), (5, 0, 3),
]


def sigmoid(values):
    return 0.5 + 0.5 * jnp.tanh(0.5 * values)


def slope(values):
    sig = sigmoid(values)
    return sig * (1.0 + values * (1.0 - sig))


def shifted(values, offset):
    column = lax.broadcasted_iota(jnp.int32, values.shape, 1)
    if offset > 0:
        return jnp.where(column < LANES - 1, pltpu.roll(values, LANES - 1, 1), 0.0)
    return jnp.where(column > 0, pltpu.roll(values, 1, 1), 0.0)


def lanes_at(start, size):
    return pl.ds(pl.multiple_of(start, LANES), size)


def rows_at(start, size):
    return pl.ds(pl.multiple_of(start, 16), size)


def unit_rows(channels, groups, places):
    total = 3 * channels * channels // LANES
    return -(-total // (2 * groups * places * 16)) * 16


def stages_of(groups):
    return groups.bit_length() - 1


def scratch_of(frames, height, channels, groups, places):
    fw = frames * LANES
    cols = height * fw
    taps = 3 * channels
    unit = unit_rows(channels, groups, places)
    piece = places * unit
    half = groups * piece
    dma = pltpu.SemaphoreType.DMA
    return {
        "u": pltpu.VMEM((frames, height, channels, LANES), BF16),
        "m1": pltpu.VMEM((channels, cols), BF16),
        "hid": pltpu.VMEM((2, channels, cols), BF16),
        "xs": pltpu.VMEM((2, taps, cols + 2 * fw), BF16),
        "ghs": pltpu.VMEM((2, taps, cols + 2 * fw), BF16),
        "act2": pltpu.VMEM((2, taps, cols), BF16),
        "gs": pltpu.VMEM((2, taps, cols), BF16),
        "conv": pltpu.VMEM((channels, cols), F32),
        "ga": pltpu.VMEM((channels, cols), F32),
        "wr": pltpu.VMEM((2, 3, taps, channels), BF16),
        "tr": pltpu.VMEM((2, taps, channels), BF16),
        "ws": pltpu.VMEM((2, 3, channels, taps), BF16),
        "ts": pltpu.VMEM((2, channels, taps), BF16),
        "grow": pltpu.VMEM((2, 1, channels), F32),
        "gcol": pltpu.VMEM((2, channels, LANES), F32),
        "ggain": pltpu.VMEM((2, channels, LANES), F32),
        "g": pltpu.VMEM((2, BANDS, 2 * half, LANES), BF16),
        "pair": pltpu.VMEM((2, BANDS, half, LANES), BF16),
        "got": pltpu.VMEM((2, BANDS, half - unit, LANES), BF16),
        "done": pltpu.VMEM((2, BANDS, half // 2, LANES), BF16),
        "gain_now": pltpu.VMEM((3, 8, channels), F32),
        "gain_pair": pltpu.VMEM((8, channels), F32),
        "gain_dp": pltpu.VMEM((groups - 1, 8, channels), F32),
        "gain_sp": pltpu.VMEM((places - 1, 8, channels), F32),
        "in_sem": dma((frames,)),
        "own_sem": dma((5,)),
        "out_sem": dma((5,)),
        "there_sem": dma((5,)),
        "gout_sem": dma((3,)),
        "halo_send": dma((2, 2, 2, frames)),
        "halo_recv": dma((2, 2, 2, frames)),
        "send": dma((2 * stages_of(groups * places) + 1, 2, BANDS)),
        "recv": dma((2 * stages_of(groups * places) + 1, 2, BANDS)),
        "keep": dma((2, BANDS)),
        "gain_send": dma((3,)),
        "gain_recv": dma((3,)),
    }


def step_kernel(names, clips, outgrad, gain, w, t, whole, gain_out, *refs):
    v = types.SimpleNamespace(**dict(zip(names, refs)))
    _, frames, height, channels, _ = clips.shape
    fw = frames * LANES
    cols = height * fw
    pairs = frames // 2
    me = lax.axis_index("segment")
    group, groups = lax.axis_index("dp"), lax.axis_size("dp")
    place, places = lax.axis_index("space"), lax.axis_size("space")
    has_up, has_down = place > 0, place < places - 1
    other = {"segment": 1 - me}
    dp_peers = [{"dp": (group + k) % groups} for k in range(1, groups)]
    cross_peers = [
        {"dp": (group + k) % groups, "segment": 1 - me} for k in range(1, groups)
    ]
    sp_peers = [{"space": (place + k) % places} for k in range(1, places)]
    center = slice(channels, 2 * channels)

    def remote(src, dst, send, recv, target):
        return pltpu.make_async_remote_copy(
            src_ref=src, dst_ref=dst, send_sem=send, recv_sem=recv,
            device_id=target, device_id_type=MESH,
        )

    barrier = pltpu.get_barrier_semaphore()
    cross_z = {"space": place + 1 - 2 * (place % 2), "segment": 1 - me}
    partners = [other] + dp_peers + cross_peers + sp_peers + [cross_z]
    for target in partners:
        pl.semaphore_signal(barrier, inc=1, device_id=target, device_id_type=MESH)

    def clip_copy(f):
        return pltpu.make_async_copy(clips.at[me, f], v.u.at[f], v.in_sem.at[f])

    for f in range(frames):
        clip_copy(f).start()
    moves = [(gain, v.grow)] + [(w.at[tap], v.wr.at[:, tap]) for tap in (1, 0, 2)] + [(t, v.tr)]
    own_copies = [
        pltpu.make_async_copy(src, into.at[me], v.own_sem.at[n])
        for n, (src, into) in enumerate(moves)
    ]
    for copy in own_copies:
        copy.start()

    for row in range(height):
        first, last = row * fw, row * fw + fw - LANES
        for s in range(2):
            v.act2[s, 0:channels, first : first + LANES] = jnp.zeros((channels, LANES), BF16)
            v.act2[s, 2 * channels :, last : last + LANES] = jnp.zeros((channels, LANES), BF16)
            v.gs[s, 0:channels, last : last + LANES] = jnp.zeros((channels, LANES), BF16)
            v.gs[s, 2 * channels :, first : first + LANES] = jnp.zeros((channels, LANES), BF16)

    @pl.when(jnp.logical_not(has_up))
    def _():
        for s in range(2):
            v.xs[s, center, 0:fw] = jnp.zeros((channels, fw), BF16)
            v.ghs[s, center, 0:fw] = jnp.zeros((channels, fw), BF16)

    @pl.when(jnp.logical_not(has_down))
    def _():
        for s in range(2):
            v.xs[s, center, cols + fw :] = jnp.zeros((channels, fw), BF16)
            v.ghs[s, center, cols + fw :] = jnp.zeros((channels, fw), BF16)

    used = 3 * channels * channels // LANES
    if used < v.g.shape[2]:
        for s in range(2):
            for band in range(BANDS):
                v.g[s, band, used:] = jnp.zeros((v.g.shape[2] - used, LANES), BF16)
    v.ggain[...] = jnp.zeros(v.ggain.shape, F32)

    pl.semaphore_wait(barrier, len(partners))
    there = [
        remote(src, into.at[me], v.out_sem.at[n], v.there_sem.at[n], other)
        for n, (src, into) in enumerate(moves)
    ]
    for copy in there:
        copy.start()
    for k in range(3):
        for f in range(frames):
            at = f + k - 1
            if 0 <= at < frames:
                for row in range(height):
                    lane = row * fw + at * LANES
                    pltpu.make_async_copy(
                        outgrad.at[me, f, row],
                        v.gs.at[1, k * channels : (k + 1) * channels, lane : lane + LANES],
                        v.gout_sem.at[k],
                    ).start()

    def wait_outgrad():
        for k in range(3):
            size = height * (frames - (k != 1)) * LANES
            ref = v.gs.at[1, k * channels : (k + 1) * channels, 0:size]
            pltpu.make_async_copy(ref, ref, v.gout_sem.at[k]).wait()

    def have(n):
        own_copies[n].wait()
        there[n].wait_recv()

    def put_row(store, s, row, f, values, reverse, own):
        lane = lanes_at(row * fw + f * LANES, LANES)
        for tap in range(3):
            offset = 1 - tap if reverse else tap - 1
            rows = slice(tap * channels, (tap + 1) * channels)
            if offset:
                store[s, rows, lane] = shifted(values, offset).astype(BF16)
            elif own:
                store[s, rows, lane] = values.astype(BF16)

    def put_frames(store, s, row, f, tile, sign):
        for k in (1, 0, 2):
            at = f + sign * (k - 1)

            def put(k=k, at=at):
                lane = lanes_at(row * fw + at * LANES, LANES)
                store[s, k * channels : (k + 1) * channels, lane] = tile

            if k == 1:
                put()
            else:
                pl.when((at >= 0) & (at < frames))(put)

    def halo_copy(store, kind, s, f, down):
        from_row, into_row = (height, 0) if down else (1, height + 1)
        return remote(
            store.at[s, center, lanes_at(from_row * fw + f * LANES, LANES)],
            store.at[s, center, lanes_at(into_row * fw + f * LANES, LANES)],
            v.halo_send.at[kind, s, down, f],
            v.halo_recv.at[kind, s, down, f],
            {"space": place + 1} if down else {"space": place - 1},
        )

    def halo_start(store, kind, s, f):
        pl.when(has_up)(lambda: halo_copy(store, kind, s, f, 0).start())
        pl.when(has_down)(lambda: halo_copy(store, kind, s, f, 1).start())

    def halo_take(store, kind, s, f, reverse):
        pl.when(has_up)(lambda: halo_copy(store, kind, s, f, 1).wait_recv())
        pl.when(has_down)(lambda: halo_copy(store, kind, s, f, 0).wait_recv())
        for row in (0, height + 1):
            lane = lanes_at(row * fw + f * LANES, LANES)
            values = store[s, center, lane].astype(F32)
            put_row(store, s, row, f, values, reverse, False)

    def halo_sent(store, kind, s):
        def body(f, _):
            pl.when(has_up)(lambda: halo_copy(store, kind, s, f, 0).wait_send())
            pl.when(has_down)(lambda: halo_copy(store, kind, s, f, 1).wait_send())
            return 0

        lax.fori_loop(0, frames, body, 0)

    def conv_own(store, s, reverse, taps=(1, 0, 2)):
        slot = 1 - s if reverse else s
        for tap in taps:
            shift = (1 - tap if reverse else tap - 1) * fw
            first, last = max(0, -shift), min(cols, cols - shift)
            values = jnp.dot(
                v.ws[slot, tap], store[s, :, fw + first + shift : fw + last + shift],
                preferred_element_type=F32,
            )
            if tap == 1:
                v.conv[...] = values
            else:
                v.conv[:, first:last] += values

    def conv_rest(store, s, row, p, reverse):
        above, below = (2, 0) if reverse else (0, 2)
        slot = 1 - s if reverse else s
        wide = 2 * LANES
        total = v.conv[:, lanes_at(row * fw + p * wide, wide)]
        if row == 0:
            total += jnp.dot(
                v.ws[slot, above], store[s, :, lanes_at(p * wide, wide)],
                preferred_element_type=F32,
            )
        if row == height - 1:
            total += jnp.dot(
                v.ws[slot, below], store[s, :, lanes_at(cols + fw + p * wide, wide)],
                preferred_element_type=F32,
            )
        return total

    def norm(s, merged):
        scale = lax.rsqrt(jnp.mean(merged * merged, axis=0, keepdims=True) + EPS)
        return scale, merged * scale * v.gcol[s]

    def activate(s, row, f, merged):
        _, pre = norm(s, merged)
        put_row(v.xs, s, row + 1, f, pre * sigmoid(pre), False, True)

    def hidden_of(s):
        def body(p, _):
            for q in range(2):
                halo_take(v.xs, 0, s, 2 * p + q, False)
            for row in range(height):
                hidden = conv_rest(v.xs, s, row, p, False).astype(BF16)
                v.hid[s, :, lanes_at(row * fw + p * 2 * LANES, 2 * LANES)] = hidden
                wide = hidden.astype(F32)
                act = (wide * sigmoid(wide)).astype(BF16)
                for q in range(2):
                    tile = act[:, q * LANES : (q + 1) * LANES]
                    put_frames(v.act2, s, row, 2 * p + q, tile, -1)
            return 0

        lax.fori_loop(0, pairs, body, 0)

    def transpose_weights(s):
        def body(tap, _):
            v.ws[s, tap] = v.wr[s, tap].T
            return 0

        lax.fori_loop(0, 3, body, 0)

    def join_weights(s):
        def body(tap, _):
            for j in range(3):
                own = slice(j * channels, (j + 1) * channels)
                v.ws[1 - s, tap, :, own] = v.wr[s, tap, own]
            return 0

        lax.fori_loop(0, 3, body, 0)
        for j in range(3):
            own = slice(j * channels, (j + 1) * channels)
            v.ts[1 - s, :, own] = v.tr[s, own]

    unit = unit_rows(channels, groups, places)
    piece = places * unit
    half = groups * piece
    count = stages_of(groups)

    def route_of(stages):
        found = types.SimpleNamespace(n=len(stages), bits=[], mates=[], lows=[me * half])
        for i, (axis, index, distance) in enumerate(stages):
            bit = (index // distance) % 2
            found.bits.append(bit)
            found.mates.append({axis: index + (1 - 2 * bit) * distance})
            found.lows.append(found.lows[i] + bit * (half // 2 ** (i + 1)))
        return found

    by_dp = [
        ("dp", group, jnp.where(me == 0, 2**i, 2 ** ((i + 1) % count))) for i in range(count)
    ]
    by_z = [("space", place, 2**i) for i in range(stages_of(places))]
    routes = {
        "direct": route_of(by_dp), "line": route_of(by_dp + by_z), "z": route_of(by_z + by_dp),
        "mid": route_of(by_dp[:1] + by_z + by_dp[1:]),
    }
    route_dp = routes["direct"]
    SP, BACK_SP = 1 + count, 2 + count

    def route(s, band):
        return routes[ROUTES[s][band]]

    def sems(stage, s, band):
        return v.send.at[stage, s, band], v.recv.at[stage, s, band]

    def halving_sems(s, band, i):
        return sems(1 + i, s, band)

    def back_sems(s, band, i):
        r = route(s, band)
        return sems(BACK_SP + i if r is route_dp else r.n + i, s, band)

    def home_sems(s, band):
        r = route(s, band)
        return sems(2 * r.n + 2 if r is route_dp else 2 * r.n, s, band)

    def got_at(i):
        size = half // 2 ** (i + 1)
        return slice(half - 2 * size, half - size)

    def got_sp(n):
        return slice(half - piece + (n - 1) * unit, half - piece + n * unit)

    def pair_copy(s, band):
        return remote(
            v.g.at[s, band, rows_at((1 - me) * half, half)], v.pair.at[s, band],
            *sems(0, s, band), other,
        )

    def halving_copy(s, band, i):
        r = route(s, band)
        size = half // 2 ** (i + 1)
        return remote(
            v.g.at[s, band, rows_at(r.lows[i] + (1 - r.bits[i]) * size, size)],
            v.got.at[s, band, got_at(i)], *halving_sems(s, band, i), r.mates[i],
        )

    def all_sp(stage, s, band):
        ref = v.got.at[s, band, half - piece : half - unit]
        return remote(ref, ref, *sems(stage, s, band), sp_peers[0])

    def back_copy(s, band, i):
        r = route(s, band)
        size = half // 2 ** (i + 1)
        at = rows_at(r.lows[i + 1] - r.lows[1], size)
        return remote(
            v.done.at[s, band, at], v.done.at[s, band, at],
            *back_sems(s, band, i), r.mates[i],
        )

    def home_copy(s, band, target):
        return remote(
            v.done.at[s, band], whole.at[band, rows_at(route(s, band).lows[1], half // 2)],
            *home_sems(s, band), target,
        )

    def keep_copy(s, band):
        return pltpu.make_async_copy(
            v.done.at[s, band], whole.at[band, rows_at(route(s, band).lows[1], half // 2)],
            v.keep.at[s, band],
        )

    def go_home(s, band):
        mate = route(s, band).mates[0]

        @pl.when(me == s)
        def _():
            home_copy(s, band, mate).start()
            keep_copy(s, band).start()

        @pl.when(me != s)
        def _():
            home_copy(s, band, {**mate, "segment": 1 - me}).start()
            home_copy(s, band, other).start()

    def send_back(s, band, i):
        if i > 0:
            back_copy(s, band, i).start()
        else:
            go_home(s, band)

    def step(k, s, band):
        r = route(s, band)
        direct = r is route_dp
        if k <= r.n:
            if k == 0:
                pair_copy(s, band).wait_recv()
                arrived = v.pair[s, band]
            else:
                halving_copy(s, band, k - 1).wait_recv()
                arrived = v.got[s, band, got_at(k - 1)]
            size = half // 2**k
            own = rows_at(r.lows[k], size)
            total = (v.g[s, band, own].astype(F32) + arrived.astype(F32)).astype(BF16)
            if k < r.n:
                v.g[s, band, own] = total
                halving_copy(s, band, k).start()
            elif direct:
                v.g[s, band, own] = total
                for n in range(1, places):
                    unit_at = r.lows[k] + ((place + n) % places) * unit
                    remote(
                        v.g.at[s, band, rows_at(unit_at, unit)],
                        v.got.at[s, band, got_sp(n)], *sems(SP, s, band), sp_peers[n - 1],
                    ).start()
            else:
                v.done[s, band, rows_at(r.lows[k] - r.lows[1], size)] = total
                send_back(s, band, k - 1)
        elif direct and k == r.n + 1:
            all_sp(SP, s, band).wait_recv()
            total = v.g[s, band, rows_at(r.lows[r.n] + place * unit, unit)].astype(F32)
            for n in range(1, places):
                total += v.got[s, band, got_sp(n)].astype(F32)
            own = rows_at(r.lows[r.n] - r.lows[1] + place * unit, unit)
            v.done[s, band, own] = total.astype(BF16)
            for n in range(1, places):
                remote(
                    v.done.at[s, band, own], v.done.at[s, band, own],
                    *sems(BACK_SP, s, band), sp_peers[n - 1],
                ).start()
        elif direct and k == r.n + 2:
            all_sp(BACK_SP, s, band).wait_recv()
            send_back(s, band, r.n - 1)
        else:
            i = 2 * r.n + (2 if direct else 0) - k
            back_copy(s, band, i).wait_recv()
            send_back(s, band, i - 1)

    def step_home(s, band):
        @pl.when(me == s)
        def _():
            keep_copy(s, band).wait()
            ref = whole.at[band, 0 : 3 * (half // 2)]
            remote(ref, ref, *home_sems(s, band), other).wait_recv()

    def wait_sends(s, band):
        r = route(s, band)
        pair_copy(s, band).wait_send()
        for i in range(r.n):
            halving_copy(s, band, i).wait_send()
        if r is route_dp:
            all_sp(SP, s, band).wait_send()
            all_sp(BACK_SP, s, band).wait_send()
        for i in range(1, r.n):
            back_copy(s, band, i).wait_send()

        @pl.when(me == s)
        def _():
            ref = whole.at[band, 0 : half // 2]
            remote(ref, ref, *home_sems(s, band), other).wait_send()

        @pl.when(me != s)
        def _():
            ref = whole.at[band, 0:half]
            remote(ref, ref, *home_sems(s, band), other).wait_send()

    def meanwhile(point, turn=None):
        if turn is None:
            for each in DURING[point]:
                step(*each)
            return
        for n, steps in enumerate(DURING[point]):

            @pl.when(turn == n)
            def _(steps=steps):
                for each in steps:
                    step(*each)

    def store_band(s, band, j, values):
        tiles, cut = channels // LANES, channels // 2
        base = j * (channels * channels // LANES)
        for n in range(tiles):
            v.g[s, band, base + n * channels : base + (n + 1) * channels] = values[
                :, n * LANES : (n + 1) * LANES
            ].astype(BF16)
        last = values[:, tiles * LANES :]
        v.g[s, band, base + tiles * channels : base + tiles * channels + cut] = jnp.concatenate(
            [last[:cut], last[cut:]], axis=1
        ).astype(BF16)

    def grads_of(s):
        for j in range(3):
            own = slice(j * channels, (j + 1) * channels)
            store_band(
                s, 0, j,
                lax.dot_general(v.act2[s, own], v.gs[s, center], NT, preferred_element_type=F32),
            )
        pair_copy(s, 0).start()

        def body(i, _):
            for j in range(3):
                own = slice(j * channels, (j + 1) * channels)
                store_band(
                    s, 1 + i, j,
                    lax.dot_general(
                        v.xs[s, own, lanes_at(i * fw, cols)],
                        v.ghs[s, center, fw : fw + cols], NT, preferred_element_type=F32,
                    ),
                )
            pair_copy(s, 1 + i).start()
            meanwhile("grads1" if s else "grads0", i)
            return 0

        lax.fori_loop(0, 3, body, 0)

    def through_time(s):
        v.ga[...] = jnp.dot(v.ts[1 - s], v.gs[s], preferred_element_type=F32)

    def ghidden_of(s):
        def body(f, _):
            for row in range(height):
                lane = lanes_at(row * fw + f * LANES, LANES)
                gh = v.ga[:, lane] * slope(v.hid[s, :, lane].astype(F32))
                if s == 0:
                    gh = gh + v.gs[s, center, lane].astype(F32)
                put_row(v.ghs, s, row + 1, f, gh, True, True)
            halo_start(v.ghs, 1, s, f)
            return 0

        lax.fori_loop(0, frames, body, 0)

    def input_grads(s, p):
        for q in range(2):
            halo_take(v.ghs, 1, s, 2 * p + q, True)
        for row in range(height):
            total = conv_rest(v.ghs, s, row, p, True)
            for q in range(2):
                f = 2 * p + q
                lane = lanes_at(row * fw + f * LANES, LANES)
                merged = (v.m1[:, lane] if s else v.u[f, row]).astype(F32)
                scale, pre = norm(s, merged)
                gpre = total[:, q * LANES : (q + 1) * LANES] * slope(pre)
                v.ggain[s] += gpre * merged * scale
                if s:
                    weighted = gpre * v.gcol[s]
                    gm = weighted * scale - merged * (scale * scale * scale) * jnp.mean(
                        weighted * merged, axis=0, keepdims=True
                    )
                    gin = (v.gs[s, center, lane].astype(F32) + gm).astype(BF16)
                    put_frames(v.gs, 0, row, f, gin, 1)

    have(0)
    for s in range(2):
        v.gcol[s] = jnp.broadcast_to(v.grow[s], (LANES, channels)).T

    def enter(f, _):
        clip_copy(f).wait()
        for row in range(height):
            activate(0, row, f, v.u[f, row].astype(F32))
        halo_start(v.xs, 0, 0, f)
        return 0

    lax.fori_loop(0, frames, enter, 0)
    for n, tap in ((1, 1), (2, 0), (3, 2)):
        have(n)
        v.ws[0, tap] = v.wr[0, tap].T
        conv_own(v.xs, 0, False, (tap,))
    have(4)
    v.ts[0] = v.tr[0].T
    transpose_weights(1)
    hidden_of(0)

    def pass_on(p, _):
        for row in range(height):
            at = row * fw + p * 2 * LANES
            mixed = jnp.dot(
                v.ts[0], v.act2[0, :, lanes_at(at, 2 * LANES)], preferred_element_type=F32
            )
            for q in range(2):
                f = 2 * p + q
                lane = lanes_at(at + q * LANES, LANES)
                out = v.u[f, row].astype(F32) + mixed[:, q * LANES : (q + 1) * LANES]
                out = out.astype(BF16).astype(F32)
                merged = (out + v.hid[0, :, lane].astype(F32)).astype(BF16)
                v.m1[:, lane] = merged
                activate(1, row, f, merged.astype(F32))
        for q in range(2):
            halo_start(v.xs, 0, 1, 2 * p + q)
        return 0

    lax.fori_loop(0, pairs, pass_on, 0)
    conv_own(v.xs, 1, False)
    join_weights(1)
    wait_outgrad()
    through_time(1)
    hidden_of(1)

    ghidden_of(1)
    grads_of(1)
    join_weights(0)
    meanwhile("joined")
    conv_own(v.ghs, 1, True)
    meanwhile("conv1")

    def back_up(p, _):
        input_grads(1, p)
        meanwhile("up", p)
        return 0

    lax.fori_loop(0, pairs, back_up, 0)

    through_time(0)
    meanwhile("time0")
    ghidden_of(0)
    meanwhile("ghidden0")
    grads_of(0)

    def gain_copy(stage, n=None):
        now = v.gain_now.at[stage]
        into = (v.gain_pair, v.gain_dp, v.gain_sp)[stage]
        peers = ([other], dp_peers, sp_peers)[stage]
        if n is None:
            now = into
        elif stage:
            into = into.at[n]
        return remote(now, into, v.gain_send.at[stage], v.gain_recv.at[stage], peers[n or 0])

    def gain_step(stage):
        if stage == 0:
            ones = jnp.ones((8, LANES), F32)
            sums = [
                lax.dot_general(
                    ones, v.ggain[s], NT, precision=lax.Precision.HIGHEST,
                    preferred_element_type=F32,
                )
                for s in range(2)
            ]
            line = lax.broadcasted_iota(jnp.int32, sums[0].shape, 0)
            total = jnp.where(line == 0, sums[0], sums[1])
        else:
            gain_copy(stage - 1).wait_recv()
            total = v.gain_now[stage - 1]
            if stage == 1:
                total += v.gain_pair[...]
            else:
                got = (v.gain_dp, v.gain_sp)[stage - 2]
                for n in range(got.shape[0]):
                    total += got[n]
        if stage == 3:
            gain_out[...] = total
            return
        v.gain_now[stage] = total
        for n in range((1, groups - 1, places - 1)[stage]):
            gain_copy(stage, n).start()

    for each in LAST:
        if each == "conv":
            conv_own(v.ghs, 0, True)
        elif each in ("rest0", "rest1"):
            input_grads(0, int(each[-1]))
        elif isinstance(each, str):
            gain_step(int(each[-1]))
        else:
            step(*each)
    for copy in there:
        copy.wait_send()
    for s in range(2):
        halo_sent(v.xs, 0, s)
        halo_sent(v.ghs, 1, s)
        for band in range(BANDS):
            wait_sends(s, band)
    for stage in range(3):
        gain_copy(stage).wait_send()
    for s in range(2):
        for band in range(BANDS):
            step_home(s, band)


def unpack_kernel(packed, gains, conv, time, gain):
    band = pl.program_id(0)
    channels = conv.shape[1]
    tiles, cut = channels // LANES, channels // 2

    def unpack(into):
        for j in range(3):
            base = j * (channels * channels // LANES)
            rows = slice(j * channels, (j + 1) * channels)
            for n in range(tiles):
                into[rows, n * LANES : (n + 1) * LANES] = packed[
                    0, base + n * channels : base + (n + 1) * channels
                ].astype(F32)
            last = packed[0, base + tiles * channels : base + tiles * channels + cut].astype(F32)
            into[j * channels : j * channels + cut, tiles * LANES :] = last[:, :64]
            into[j * channels + cut : (j + 1) * channels, tiles * LANES :] = last[:, 64:]

    @pl.when(band == 0)
    def _():
        unpack(time)
        me = lax.axis_index("segment")
        gain[...] = jnp.where(me == 0, gains[0:1], gains[1:2])

    @pl.when(band > 0)
    def _():
        unpack(conv)


def body(video_clips, output_grad, norm_gain, conv_weight, time_weight):
    channels = conv_weight.shape[3]
    clips, frames, height, _, width = video_clips.shape
    assert clips == 2 and width == LANES and channels % LANES == 64 and frames == 4
    groups, places = lax.axis_size("dp"), lax.axis_size("space")
    taps = 3 * channels
    scratch = scratch_of(frames, height, channels, groups, places)
    rows = 2 * groups * places * unit_rows(channels, groups, places)
    packed, gains = pl.pallas_call(
        functools.partial(step_kernel, tuple(scratch)),
        out_shape=[
            jax.ShapeDtypeStruct((BANDS, rows, LANES), BF16),
            jax.ShapeDtypeStruct((8, channels), F32),
        ],
        in_specs=[ANY, ANY, VMEM, ANY, ANY],
        out_specs=[ANY, VMEM],
        scratch_shapes=list(scratch.values()),
        compiler_params=pltpu.CompilerParams(
            collective_id=0, has_side_effects=True, vmem_limit_bytes=LIMIT
        ),
        name="step",
    )(
        video_clips, output_grad, norm_gain,
        conv_weight.reshape(3, taps, channels), time_weight.reshape(taps, channels),
    )
    conv, time, row = pl.pallas_call(
        unpack_kernel,
        grid=(BANDS,),
        out_shape=[
            jax.ShapeDtypeStruct((3 * taps, channels), F32),
            jax.ShapeDtypeStruct((taps, channels), F32),
            jax.ShapeDtypeStruct((1, channels), F32),
        ],
        in_specs=[
            pl.BlockSpec((1, rows, LANES), lambda b: (b, 0, 0)),
            pl.BlockSpec((8, channels), lambda b: (0, 0)),
        ],
        out_specs=[
            pl.BlockSpec((taps, channels), lambda b: (jnp.maximum(b - 1, 0), 0)),
            pl.BlockSpec((taps, channels), lambda b: (0, 0)),
            pl.BlockSpec((1, channels), lambda b: (0, 0)),
        ],
        compiler_params=pltpu.CompilerParams(vmem_limit_bytes=LIMIT),
        name="unpack",
    )(packed, gains)
    return (
        conv.reshape(conv_weight.shape),
        time.reshape(time_weight.shape),
        row,
    )


def solution(mesh):
    placed = (
        P("dp", None, "space", None, None),
        P("dp", None, "space", None, None),
        P("segment", None),
        P("segment", None, None, None, None),
        P("segment", None, None, None),
    )
    return jax.shard_map(
        body,
        mesh=mesh,
        in_specs=placed,
        out_specs=(
            P("segment", None, None, None, None),
            P("segment", None, None, None),
            P("segment", None),
        ),
        check_vma=False,
    )
```

```python
import functools
import types

import jax
import jax.numpy as jnp
from jax import lax
from jax.experimental import pallas as pl
from jax.experimental.pallas import tpu as pltpu
from jax.sharding import PartitionSpec as P

EPS = 1e-06
MESH = pl.DeviceIdType.MESH
VMEM = pl.BlockSpec(memory_space=pltpu.VMEM)
ANY = pl.BlockSpec(memory_space=pl.ANY)
BF16 = jnp.bfloat16
F32 = jnp.float32
LIMIT = 65000 * 1024
NT = (((1,), (1,)), ((), ()))
LANES = 128
BANDS = 4


ROUTES = (("direct",) * 4, ("direct",) * 4)
DURING = {
    "grads1": [[(0, 1, 0)], [(0, 1, 1)], [(0, 1, 2)]],
    "joined": [],
    "conv1": [(0, 1, 3)],
    "up": [[(1, 1, 0), (1, 1, 1)], [(1, 1, 2)]],
    "time0": [(1, 1, 3)],
    "ghidden0": [(2, 1, 0)],
    "grads0": [[(2, 1, 1), (2, 1, 2)], [(0, 0, 0), (2, 1, 3)], [(0, 0, 1), (3, 1, 0)]],
}
LAST = [
    (0, 0, 2), (0, 0, 3), (3, 1, 1), "conv", (1, 0, 0), (3, 1, 2), (3, 1, 3), "rest0", (1, 0,
    1), "rest1", (1, 0, 2), (4, 1, 0), "gain0", (1, 0, 3), (4, 1, 1), (2, 0, 0), (4, 1, 2), (2,
    0, 1), "gain1", (2, 0, 2), (4, 1, 3), (5, 1, 0), (2, 0, 3), (3, 0, 0), (5, 1, 1), "gain2",
    (3, 0, 1), (5, 1, 2), (3, 0, 2), (5, 1, 3), (3, 0, 3), (4, 0, 0), "gain3", (4, 0, 1), (4, 0,
    2), (4, 0, 3), (5, 0, 0), (5, 0, 1), (5, 0, 2), (5, 0, 3),
]


def sigmoid(values):
    return 0.5 + 0.5 * jnp.tanh(0.5 * values)


def slope(values):
    sig = sigmoid(values)
    return sig * (1.0 + values * (1.0 - sig))


def shifted(values, offset):
    column = lax.broadcasted_iota(jnp.int32, values.shape, 1)
    if offset > 0:
        return jnp.where(column < LANES - 1, pltpu.roll(values, LANES - 1, 1), 0.0)
    return jnp.where(column > 0, pltpu.roll(values, 1, 1), 0.0)


def lanes_at(start, size):
    return pl.ds(pl.multiple_of(start, LANES), size)


def rows_at(start, size):
    return pl.ds(pl.multiple_of(start, 16), size)


def unit_rows(channels, groups, places):
    total = 3 * channels * channels // LANES
    return -(-total // (2 * groups * places * 16)) * 16


def stages_of(groups):
    return groups.bit_length() - 1


def scratch_of(frames, height, channels, groups, places):
    fw = frames * LANES
    cols = height * fw
    taps = 3 * channels
    unit = unit_rows(channels, groups, places)
    piece = places * unit
    half = groups * piece
    dma = pltpu.SemaphoreType.DMA
    return {
        "u": pltpu.VMEM((frames, height, channels, LANES), BF16),
        "m1": pltpu.VMEM((channels, cols), BF16),
        "hid": pltpu.VMEM((2, channels, cols), BF16),
        "xs": pltpu.VMEM((2, taps, cols + 2 * fw), BF16),
        "ghs": pltpu.VMEM((2, taps, cols + 2 * fw), BF16),
        "act2": pltpu.VMEM((2, taps, cols), BF16),
        "gs": pltpu.VMEM((2, taps, cols), BF16),
        "conv": pltpu.VMEM((channels, cols), F32),
        "ga": pltpu.VMEM((channels, cols), F32),
        "wr": pltpu.VMEM((2, 3, taps, channels), BF16),
        "tr": pltpu.VMEM((2, taps, channels), BF16),
        "ws": pltpu.VMEM((2, 3, channels, taps), BF16),
        "ts": pltpu.VMEM((2, channels, taps), BF16),
        "grow": pltpu.VMEM((2, 1, channels), F32),
        "gcol": pltpu.VMEM((2, channels, LANES), F32),
        "ggain": pltpu.VMEM((2, channels, LANES), F32),
        "g": pltpu.VMEM((2, BANDS, 2 * half, LANES), BF16),
        "pair": pltpu.VMEM((2, BANDS, half, LANES), BF16),
        "got": pltpu.VMEM((2, BANDS, half - unit, LANES), BF16),
        "done": pltpu.VMEM((2, BANDS, half // 2, LANES), BF16),
        "gain_now": pltpu.VMEM((3, 8, channels), F32),
        "gain_pair": pltpu.VMEM((8, channels), F32),
        "gain_dp": pltpu.VMEM((groups - 1, 8, channels), F32),
        "gain_sp": pltpu.VMEM((places - 1, 8, channels), F32),
        "in_sem": dma((frames,)),
        "own_sem": dma((5,)),
        "out_sem": dma((5,)),
        "there_sem": dma((5,)),
        "gout_sem": dma((3,)),
        "halo_send": dma((2, 2, 2, frames)),
        "halo_recv": dma((2, 2, 2, frames)),
        "send": dma((2 * stages_of(groups * places) + 1, 2, BANDS)),
        "recv": dma((2 * stages_of(groups * places) + 1, 2, BANDS)),
        "keep": dma((2, BANDS)),
        "gain_send": dma((3,)),
        "gain_recv": dma((3,)),
    }


def step_kernel(names, clips, outgrad, gain, w, t, whole, gain_out, *refs):
    v = types.SimpleNamespace(**dict(zip(names, refs)))
    _, frames, height, channels, _ = clips.shape
    fw = frames * LANES
    cols = height * fw
    pairs = frames // 2
    me = lax.axis_index("segment")
    group, groups = lax.axis_index("dp"), lax.axis_size("dp")
    place, places = lax.axis_index("space"), lax.axis_size("space")
    has_up, has_down = place > 0, place < places - 1
    other = {"segment": 1 - me}
    dp_peers = [{"dp": (group + k) % groups} for k in range(1, groups)]
    cross_peers = [
        {"dp": (group + k) % groups, "segment": 1 - me} for k in range(1, groups)
    ]
    sp_peers = [{"space": (place + k) % places} for k in range(1, places)]
    center = slice(channels, 2 * channels)

    def remote(src, dst, send, recv, target):
        return pltpu.make_async_remote_copy(
            src_ref=src, dst_ref=dst, send_sem=send, recv_sem=recv,
            device_id=target, device_id_type=MESH,
        )

    barrier = pltpu.get_barrier_semaphore()
    cross_z = {"space": place + 1 - 2 * (place % 2), "segment": 1 - me}
    partners = [other] + dp_peers + cross_peers + sp_peers + [cross_z]
    for target in partners:
        pl.semaphore_signal(barrier, inc=1, device_id=target, device_id_type=MESH)

    def clip_copy(f):
        return pltpu.make_async_copy(clips.at[me, f], v.u.at[f], v.in_sem.at[f])

    for f in range(frames):
        clip_copy(f).start()
    moves = [(gain, v.grow)] + [(w.at[tap], v.wr.at[:, tap]) for tap in (1, 0, 2)] + [(t, v.tr)]
    own_copies = [
        pltpu.make_async_copy(src, into.at[me], v.own_sem.at[n])
        for n, (src, into) in enumerate(moves)
    ]
    for copy in own_copies:
        copy.start()

    for row in range(height):
        first, last = row * fw, row * fw + fw - LANES
        for s in range(2):
            v.act2[s, 0:channels, first : first + LANES] = jnp.zeros((channels, LANES), BF16)
            v.act2[s, 2 * channels :, last : last + LANES] = jnp.zeros((channels, LANES), BF16)
            v.gs[s, 0:channels, last : last + LANES] = jnp.zeros((channels, LANES), BF16)
            v.gs[s, 2 * channels :, first : first + LANES] = jnp.zeros((channels, LANES), BF16)

    @pl.when(jnp.logical_not(has_up))
    def _():
        for s in range(2):
            v.xs[s, center, 0:fw] = jnp.zeros((channels, fw), BF16)
            v.ghs[s, center, 0:fw] = jnp.zeros((channels, fw), BF16)

    @pl.when(jnp.logical_not(has_down))
    def _():
        for s in range(2):
            v.xs[s, center, cols + fw :] = jnp.zeros((channels, fw), BF16)
            v.ghs[s, center, cols + fw :] = jnp.zeros((channels, fw), BF16)

    used = 3 * channels * channels // LANES
    if used < v.g.shape[2]:
        for s in range(2):
            for band in range(BANDS):
                v.g[s, band, used:] = jnp.zeros((v.g.shape[2] - used, LANES), BF16)
    v.ggain[...] = jnp.zeros(v.ggain.shape, F32)

    pl.semaphore_wait(barrier, len(partners))
    there = [
        remote(src, into.at[me], v.out_sem.at[n], v.there_sem.at[n], other)
        for n, (src, into) in enumerate(moves)
    ]
    for copy in there:
        copy.start()
    for k in range(3):
        for f in range(frames):
            at = f + k - 1
            if 0 <= at < frames:
                for row in range(height):
                    lane = row * fw + at * LANES
                    pltpu.make_async_copy(
                        outgrad.at[me, f, row],
                        v.gs.at[1, k * channels : (k + 1) * channels, lane : lane + LANES],
                        v.gout_sem.at[k],
                    ).start()

    def wait_outgrad():
        for k in range(3):
            size = height * (frames - (k != 1)) * LANES
            ref = v.gs.at[1, k * channels : (k + 1) * channels, 0:size]
            pltpu.make_async_copy(ref, ref, v.gout_sem.at[k]).wait()

    def have(n):
        own_copies[n].wait()
        there[n].wait_recv()

    def put_row(store, s, row, f, values, reverse, own):
        lane = lanes_at(row * fw + f * LANES, LANES)
        for tap in range(3):
            offset = 1 - tap if reverse else tap - 1
            rows = slice(tap * channels, (tap + 1) * channels)
            if offset:
                store[s, rows, lane] = shifted(values, offset).astype(BF16)
            elif own:
                store[s, rows, lane] = values.astype(BF16)

    def put_frames(store, s, row, f, tile, sign):
        for k in (1, 0, 2):
            at = f + sign * (k - 1)

            def put(k=k, at=at):
                lane = lanes_at(row * fw + at * LANES, LANES)
                store[s, k * channels : (k + 1) * channels, lane] = tile

            if k == 1:
                put()
            else:
                pl.when((at >= 0) & (at < frames))(put)

    def halo_copy(store, kind, s, f, down):
        from_row, into_row = (height, 0) if down else (1, height + 1)
        return remote(
            store.at[s, center, lanes_at(from_row * fw + f * LANES, LANES)],
            store.at[s, center, lanes_at(into_row * fw + f * LANES, LANES)],
            v.halo_send.at[kind, s, down, f],
            v.halo_recv.at[kind, s, down, f],
            {"space": place + 1} if down else {"space": place - 1},
        )

    def halo_start(store, kind, s, f):
        pl.when(has_up)(lambda: halo_copy(store, kind, s, f, 0).start())
        pl.when(has_down)(lambda: halo_copy(store, kind, s, f, 1).start())

    def halo_take(store, kind, s, f, reverse):
        pl.when(has_up)(lambda: halo_copy(store, kind, s, f, 1).wait_recv())
        pl.when(has_down)(lambda: halo_copy(store, kind, s, f, 0).wait_recv())
        for row in (0, height + 1):
            lane = lanes_at(row * fw + f * LANES, LANES)
            values = store[s, center, lane].astype(F32)
            put_row(store, s, row, f, values, reverse, False)

    def halo_sent(store, kind, s):
        def body(f, _):
            pl.when(has_up)(lambda: halo_copy(store, kind, s, f, 0).wait_send())
            pl.when(has_down)(lambda: halo_copy(store, kind, s, f, 1).wait_send())
            return 0

        lax.fori_loop(0, frames, body, 0)

    def conv_own(store, s, reverse, taps=(1, 0, 2)):
        slot = 1 - s if reverse else s
        for tap in taps:
            shift = (1 - tap if reverse else tap - 1) * fw
            first, last = max(0, -shift), min(cols, cols - shift)
            values = jnp.dot(
                v.ws[slot, tap], store[s, :, fw + first + shift : fw + last + shift],
                preferred_element_type=F32,
            )
            if tap == 1:
                v.conv[...] = values
            else:
                v.conv[:, first:last] += values

    def conv_rest(store, s, row, p, reverse):
        above, below = (2, 0) if reverse else (0, 2)
        slot = 1 - s if reverse else s
        wide = 2 * LANES
        total = v.conv[:, lanes_at(row * fw + p * wide, wide)]
        if row == 0:
            total += jnp.dot(
                v.ws[slot, above], store[s, :, lanes_at(p * wide, wide)],
                preferred_element_type=F32,
            )
        if row == height - 1:
            total += jnp.dot(
                v.ws[slot, below], store[s, :, lanes_at(cols + fw + p * wide, wide)],
                preferred_element_type=F32,
            )
        return total

    def norm(s, merged):
        scale = lax.rsqrt(jnp.mean(merged * merged, axis=0, keepdims=True) + EPS)
        return scale, merged * scale * v.gcol[s]

    def activate(s, row, f, merged):
        _, pre = norm(s, merged)
        put_row(v.xs, s, row + 1, f, pre * sigmoid(pre), False, True)

    def hidden_of(s):
        def body(p, _):
            for q in range(2):
                halo_take(v.xs, 0, s, 2 * p + q, False)
            for row in range(height):
                hidden = conv_rest(v.xs, s, row, p, False).astype(BF16)
                v.hid[s, :, lanes_at(row * fw + p * 2 * LANES, 2 * LANES)] = hidden
                wide = hidden.astype(F32)
                act = (wide * sigmoid(wide)).astype(BF16)
                for q in range(2):
                    tile = act[:, q * LANES : (q + 1) * LANES]
                    put_frames(v.act2, s, row, 2 * p + q, tile, -1)
            return 0

        lax.fori_loop(0, pairs, body, 0)

    def transpose_weights(s):
        def body(tap, _):
            v.ws[s, tap] = v.wr[s, tap].T
            return 0

        lax.fori_loop(0, 3, body, 0)

    def join_weights(s):
        def body(tap, _):
            for j in range(3):
                own = slice(j * channels, (j + 1) * channels)
                v.ws[1 - s, tap, :, own] = v.wr[s, tap, own]
            return 0

        lax.fori_loop(0, 3, body, 0)
        for j in range(3):
            own = slice(j * channels, (j + 1) * channels)
            v.ts[1 - s, :, own] = v.tr[s, own]

    unit = unit_rows(channels, groups, places)
    piece = places * unit
    half = groups * piece
    count = stages_of(groups)

    def route_of(stages):
        found = types.SimpleNamespace(n=len(stages), bits=[], mates=[], lows=[me * half])
        for i, (axis, index, distance) in enumerate(stages):
            bit = (index // distance) % 2
            found.bits.append(bit)
            found.mates.append({axis: index + (1 - 2 * bit) * distance})
            found.lows.append(found.lows[i] + bit * (half // 2 ** (i + 1)))
        return found

    by_dp = [
        ("dp", group, jnp.where(me == 0, 2**i, 2 ** ((i + 1) % count))) for i in range(count)
    ]
    by_z = [("space", place, 2**i) for i in range(stages_of(places))]
    routes = {
        "direct": route_of(by_dp), "line": route_of(by_dp + by_z), "z": route_of(by_z + by_dp),
        "mid": route_of(by_dp[:1] + by_z + by_dp[1:]),
    }
    route_dp = routes["direct"]
    SP, BACK_SP = 1 + count, 2 + count

    def route(s, band):
        return routes[ROUTES[s][band]]

    def sems(stage, s, band):
        return v.send.at[stage, s, band], v.recv.at[stage, s, band]

    def halving_sems(s, band, i):
        return sems(1 + i, s, band)

    def back_sems(s, band, i):
        r = route(s, band)
        return sems(BACK_SP + i if r is route_dp else r.n + i, s, band)

    def home_sems(s, band):
        r = route(s, band)
        return sems(2 * r.n + 2 if r is route_dp else 2 * r.n, s, band)

    def got_at(i):
        size = half // 2 ** (i + 1)
        return slice(half - 2 * size, half - size)

    def got_sp(n):
        return slice(half - piece + (n - 1) * unit, half - piece + n * unit)

    def pair_copy(s, band):
        return remote(
            v.g.at[s, band, rows_at((1 - me) * half, half)], v.pair.at[s, band],
            *sems(0, s, band), other,
        )

    def halving_copy(s, band, i):
        r = route(s, band)
        size = half // 2 ** (i + 1)
        return remote(
            v.g.at[s, band, rows_at(r.lows[i] + (1 - r.bits[i]) * size, size)],
            v.got.at[s, band, got_at(i)], *halving_sems(s, band, i), r.mates[i],
        )

    def all_sp(stage, s, band):
        ref = v.got.at[s, band, half - piece : half - unit]
        return remote(ref, ref, *sems(stage, s, band), sp_peers[0])

    def back_copy(s, band, i):
        r = route(s, band)
        size = half // 2 ** (i + 1)
        at = rows_at(r.lows[i + 1] - r.lows[1], size)
        return remote(
            v.done.at[s, band, at], v.done.at[s, band, at],
            *back_sems(s, band, i), r.mates[i],
        )

    def home_copy(s, band, target):
        return remote(
            v.done.at[s, band], whole.at[band, rows_at(route(s, band).lows[1], half // 2)],
            *home_sems(s, band), target,
        )

    def keep_copy(s, band):
        return pltpu.make_async_copy(
            v.done.at[s, band], whole.at[band, rows_at(route(s, band).lows[1], half // 2)],
            v.keep.at[s, band],
        )

    def go_home(s, band):
        mate = route(s, band).mates[0]

        @pl.when(me == s)
        def _():
            home_copy(s, band, mate).start()
            keep_copy(s, band).start()

        @pl.when(me != s)
        def _():
            home_copy(s, band, {**mate, "segment": 1 - me}).start()
            home_copy(s, band, other).start()

    def send_back(s, band, i):
        if i > 0:
            back_copy(s, band, i).start()
        else:
            go_home(s, band)

    def step(k, s, band):
        r = route(s, band)
        direct = r is route_dp
        if k <= r.n:
            if k == 0:
                pair_copy(s, band).wait_recv()
                arrived = v.pair[s, band]
            else:
                halving_copy(s, band, k - 1).wait_recv()
                arrived = v.got[s, band, got_at(k - 1)]
            size = half // 2**k
            own = rows_at(r.lows[k], size)
            total = (v.g[s, band, own].astype(F32) + arrived.astype(F32)).astype(BF16)
            if k < r.n:
                v.g[s, band, own] = total
                halving_copy(s, band, k).start()
            elif direct:
                v.g[s, band, own] = total
                for n in range(1, places):
                    unit_at = r.lows[k] + ((place + n) % places) * unit
                    remote(
                        v.g.at[s, band, rows_at(unit_at, unit)],
                        v.got.at[s, band, got_sp(n)], *sems(SP, s, band), sp_peers[n - 1],
                    ).start()
            else:
                v.done[s, band, rows_at(r.lows[k] - r.lows[1], size)] = total
                send_back(s, band, k - 1)
        elif direct and k == r.n + 1:
            all_sp(SP, s, band).wait_recv()
            total = v.g[s, band, rows_at(r.lows[r.n] + place * unit, unit)].astype(F32)
            for n in range(1, places):
                total += v.got[s, band, got_sp(n)].astype(F32)
            own = rows_at(r.lows[r.n] - r.lows[1] + place * unit, unit)
            v.done[s, band, own] = total.astype(BF16)
            for n in range(1, places):
                remote(
                    v.done.at[s, band, own], v.done.at[s, band, own],
                    *sems(BACK_SP, s, band), sp_peers[n - 1],
                ).start()
        elif direct and k == r.n + 2:
            all_sp(BACK_SP, s, band).wait_recv()
            send_back(s, band, r.n - 1)
        else:
            i = 2 * r.n + (2 if direct else 0) - k
            back_copy(s, band, i).wait_recv()
            send_back(s, band, i - 1)

    def step_home(s, band):
        @pl.when(me == s)
        def _():
            keep_copy(s, band).wait()
            ref = whole.at[band, 0 : 3 * (half // 2)]
            remote(ref, ref, *home_sems(s, band), other).wait_recv()

    def wait_sends(s, band):
        r = route(s, band)
        pair_copy(s, band).wait_send()
        for i in range(r.n):
            halving_copy(s, band, i).wait_send()
        if r is route_dp:
            all_sp(SP, s, band).wait_send()
            all_sp(BACK_SP, s, band).wait_send()
        for i in range(1, r.n):
            back_copy(s, band, i).wait_send()

        @pl.when(me == s)
        def _():
            ref = whole.at[band, 0 : half // 2]
            remote(ref, ref, *home_sems(s, band), other).wait_send()

        @pl.when(me != s)
        def _():
            ref = whole.at[band, 0:half]
            remote(ref, ref, *home_sems(s, band), other).wait_send()

    def meanwhile(point, turn=None):
        if turn is None:
            for each in DURING[point]:
                step(*each)
            return
        for n, steps in enumerate(DURING[point]):

            @pl.when(turn == n)
            def _(steps=steps):
                for each in steps:
                    step(*each)

    def store_band(s, band, j, values):
        tiles, cut = channels // LANES, channels // 2
        base = j * (channels * channels // LANES)
        for n in range(tiles):
            v.g[s, band, base + n * channels : base + (n + 1) * channels] = values[
                :, n * LANES : (n + 1) * LANES
            ].astype(BF16)
        last = values[:, tiles * LANES :]
        v.g[s, band, base + tiles * channels : base + tiles * channels + cut] = jnp.concatenate(
            [last[:cut], last[cut:]], axis=1
        ).astype(BF16)

    def grads_of(s):
        for j in range(3):
            own = slice(j * channels, (j + 1) * channels)
            store_band(
                s, 0, j,
                lax.dot_general(v.act2[s, own], v.gs[s, center], NT, preferred_element_type=F32),
            )
        pair_copy(s, 0).start()

        def body(i, _):
            for j in range(3):
                own = slice(j * channels, (j + 1) * channels)
                store_band(
                    s, 1 + i, j,
                    lax.dot_general(
                        v.xs[s, own, lanes_at(i * fw, cols)],
                        v.ghs[s, center, fw : fw + cols], NT, preferred_element_type=F32,
                    ),
                )
            pair_copy(s, 1 + i).start()
            meanwhile("grads1" if s else "grads0", i)
            return 0

        lax.fori_loop(0, 3, body, 0)

    def through_time(s):
        v.ga[...] = jnp.dot(v.ts[1 - s], v.gs[s], preferred_element_type=F32)

    def ghidden_of(s):
        def body(f, _):
            for row in range(height):
                lane = lanes_at(row * fw + f * LANES, LANES)
                gh = v.ga[:, lane] * slope(v.hid[s, :, lane].astype(F32))
                if s == 0:
                    gh = gh + v.gs[s, center, lane].astype(F32)
                put_row(v.ghs, s, row + 1, f, gh, True, True)
            halo_start(v.ghs, 1, s, f)
            return 0

        lax.fori_loop(0, frames, body, 0)

    def input_grads(s, p):
        for q in range(2):
            halo_take(v.ghs, 1, s, 2 * p + q, True)
        for row in range(height):
            total = conv_rest(v.ghs, s, row, p, True)
            for q in range(2):
                f = 2 * p + q
                lane = lanes_at(row * fw + f * LANES, LANES)
                merged = (v.m1[:, lane] if s else v.u[f, row]).astype(F32)
                scale, pre = norm(s, merged)
                gpre = total[:, q * LANES : (q + 1) * LANES] * slope(pre)
                v.ggain[s] += gpre * merged * scale
                if s:
                    weighted = gpre * v.gcol[s]
                    gm = weighted * scale - merged * (scale * scale * scale) * jnp.mean(
                        weighted * merged, axis=0, keepdims=True
                    )
                    gin = (v.gs[s, center, lane].astype(F32) + gm).astype(BF16)
                    put_frames(v.gs, 0, row, f, gin, 1)

    have(0)
    for s in range(2):
        v.gcol[s] = jnp.broadcast_to(v.grow[s], (LANES, channels)).T

    def enter(f, _):
        clip_copy(f).wait()
        for row in range(height):
            activate(0, row, f, v.u[f, row].astype(F32))
        halo_start(v.xs, 0, 0, f)
        return 0

    lax.fori_loop(0, frames, enter, 0)
    for n, tap in ((1, 1), (2, 0), (3, 2)):
        have(n)
        v.ws[0, tap] = v.wr[0, tap].T
        conv_own(v.xs, 0, False, (tap,))
    have(4)
    v.ts[0] = v.tr[0].T
    transpose_weights(1)
    hidden_of(0)

    def pass_on(p, _):
        for row in range(height):
            at = row * fw + p * 2 * LANES
            mixed = jnp.dot(
                v.ts[0], v.act2[0, :, lanes_at(at, 2 * LANES)], preferred_element_type=F32
            )
            for q in range(2):
                f = 2 * p + q
                lane = lanes_at(at + q * LANES, LANES)
                out = v.u[f, row].astype(F32) + mixed[:, q * LANES : (q + 1) * LANES]
                out = out.astype(BF16).astype(F32)
                merged = (out + v.hid[0, :, lane].astype(F32)).astype(BF16)
                v.m1[:, lane] = merged
                activate(1, row, f, merged.astype(F32))
        for q in range(2):
            halo_start(v.xs, 0, 1, 2 * p + q)
        return 0

    lax.fori_loop(0, pairs, pass_on, 0)
    conv_own(v.xs, 1, False)
    join_weights(1)
    wait_outgrad()
    through_time(1)
    hidden_of(1)

    ghidden_of(1)
    grads_of(1)
    join_weights(0)
    meanwhile("joined")
    conv_own(v.ghs, 1, True)
    meanwhile("conv1")

    def back_up(p, _):
        input_grads(1, p)
        meanwhile("up", p)
        return 0

    lax.fori_loop(0, pairs, back_up, 0)

    through_time(0)
    meanwhile("time0")
    ghidden_of(0)
    meanwhile("ghidden0")
    grads_of(0)

    def gain_copy(stage, n=None):
        now = v.gain_now.at[stage]
        into = (v.gain_pair, v.gain_dp, v.gain_sp)[stage]
        peers = ([other], dp_peers, sp_peers)[stage]
        if n is None:
            now = into
        elif stage:
            into = into.at[n]
        return remote(now, into, v.gain_send.at[stage], v.gain_recv.at[stage], peers[n or 0])

    def gain_step(stage):
        if stage == 0:
            ones = jnp.ones((8, LANES), F32)
            sums = [
                lax.dot_general(
                    ones, v.ggain[s], NT, precision=lax.Precision.HIGHEST,
                    preferred_element_type=F32,
                )
                for s in range(2)
            ]
            line = lax.broadcasted_iota(jnp.int32, sums[0].shape, 0)
            total = jnp.where(line == 0, sums[0], sums[1])
        else:
            gain_copy(stage - 1).wait_recv()
            total = v.gain_now[stage - 1]
            if stage == 1:
                total += v.gain_pair[...]
            else:
                got = (v.gain_dp, v.gain_sp)[stage - 2]
                for n in range(got.shape[0]):
                    total += got[n]
        if stage == 3:
            gain_out[...] = total
            return
        v.gain_now[stage] = total
        for n in range((1, groups - 1, places - 1)[stage]):
            gain_copy(stage, n).start()

    for each in LAST:
        if each == "conv":
            conv_own(v.ghs, 0, True)
        elif each in ("rest0", "rest1"):
            input_grads(0, int(each[-1]))
        elif isinstance(each, str):
            gain_step(int(each[-1]))
        else:
            step(*each)
    for copy in there:
        copy.wait_send()
    for s in range(2):
        halo_sent(v.xs, 0, s)
        halo_sent(v.ghs, 1, s)
        for band in range(BANDS):
            wait_sends(s, band)
    for stage in range(3):
        gain_copy(stage).wait_send()
    for s in range(2):
        for band in range(BANDS):
            step_home(s, band)


def unpack_kernel(packed, gains, conv, time, gain):
    band = pl.program_id(0)
    channels = conv.shape[1]
    tiles, cut = channels // LANES, channels // 2

    def unpack(into):
        for j in range(3):
            base = j * (channels * channels // LANES)
            rows = slice(j * channels, (j + 1) * channels)
            for n in range(tiles):
                into[rows, n * LANES : (n + 1) * LANES] = packed[
                    0, base + n * channels : base + (n + 1) * channels
                ].astype(F32)
            last = packed[0, base + tiles * channels : base + tiles * channels + cut].astype(F32)
            into[j * channels : j * channels + cut, tiles * LANES :] = last[:, :64]
            into[j * channels + cut : (j + 1) * channels, tiles * LANES :] = last[:, 64:]

    @pl.when(band == 0)
    def _():
        unpack(time)
        me = lax.axis_index("segment")
        gain[...] = jnp.where(me == 0, gains[0:1], gains[1:2])

    @pl.when(band > 0)
    def _():
        unpack(conv)


def body(video_clips, output_grad, norm_gain, conv_weight, time_weight):
    channels = conv_weight.shape[3]
    clips, frames, height, _, width = video_clips.shape
    assert clips == 2 and width == LANES and channels % LANES == 64 and frames == 4
    groups, places = lax.axis_size("dp"), lax.axis_size("space")
    taps = 3 * channels
    scratch = scratch_of(frames, height, channels, groups, places)
    rows = 2 * groups * places * unit_rows(channels, groups, places)
    packed, gains = pl.pallas_call(
        functools.partial(step_kernel, tuple(scratch)),
        out_shape=[
            jax.ShapeDtypeStruct((BANDS, rows, LANES), BF16),
            jax.ShapeDtypeStruct((8, channels), F32),
        ],
        in_specs=[ANY, ANY, VMEM, ANY, ANY],
        out_specs=[ANY, VMEM],
        scratch_shapes=list(scratch.values()),
        compiler_params=pltpu.CompilerParams(
            collective_id=0, has_side_effects=True, vmem_limit_bytes=LIMIT
        ),
        name="step",
    )(
        video_clips, output_grad, norm_gain,
        conv_weight.reshape(3, taps, channels), time_weight.reshape(taps, channels),
    )
    conv, time, row = pl.pallas_call(
        unpack_kernel,
        grid=(BANDS,),
        out_shape=[
            jax.ShapeDtypeStruct((3 * taps, channels), F32),
            jax.ShapeDtypeStruct((taps, channels), F32),
            jax.ShapeDtypeStruct((1, channels), F32),
        ],
        in_specs=[
            pl.BlockSpec((1, rows, LANES), lambda b: (b, 0, 0)),
            pl.BlockSpec((8, channels), lambda b: (0, 0)),
        ],
        out_specs=[
            pl.BlockSpec((taps, channels), lambda b: (jnp.maximum(b - 1, 0), 0)),
            pl.BlockSpec((taps, channels), lambda b: (0, 0)),
            pl.BlockSpec((1, channels), lambda b: (0, 0)),
        ],
        compiler_params=pltpu.CompilerParams(vmem_limit_bytes=LIMIT),
        name="unpack",
    )(packed, gains)
    return (
        conv.reshape(conv_weight.shape),
        time.reshape(time_weight.shape),
        row,
    )


def solution(mesh):
    placed = (
        P("dp", None, "space", None, None),
        P("dp", None, "space", None, None),
        P("segment", None),
        P("segment", None, None, None, None),
        P("segment", None, None, None),
    )
    return jax.shard_map(
        body,
        mesh=mesh,
        in_specs=placed,
        out_specs=(
            P("segment", None, None, None, None),
            P("segment", None, None, None),
            P("segment", None),
        ),
        check_vma=False,
    )
```
